32 devices in a mesh: groups: 2 (over y), tile: 16 (over z, x, core).
Axes of the slice: x: 2, y: 2, z: 4, core: 2. Of those that a mesh axis runs over, the one named last changes fastest.
Arguments:
- log_demand: float32 [512, 256], P(('groups', 'tile')), parts along dimension 0, may hold values from -3 to 0
- log_capacity: float32 [32, 256], P(('groups', 'tile')), parts along dimension 0, may hold values from -1 to 1
- warm_potential: float32 [32, 256], P(('groups', 'tile')), parts along dimension 0, may hold values from -4 to 4
- facility_xy: float32 [32, 2, 256], P('groups'), parts along dimension 0, may hold values from 0 to 1472
- pair_block: int32 [512, 16], P(('groups', 'tile')), parts along dimension 0, may hold values from 0 to 15, as said below
- pair_count: int32 [512], P(('groups', 'tile')), parts along dimension 0, may hold values from 1 to 16, as said below
Outputs:
- cell_potential: float32 [512, 256], P(('groups', 'tile')), parts along dimension 0
- facility_potential: float32 [32, 256], P(('groups', 'tile')), parts along dimension 0
The draws below stay inside these ranges and needn't reach their ends.
There are 2 independent parts, one for each index of `groups`. The reference program is written for one: setup_inputs(seed, part) draws one part's arguments, and reference() takes and returns one part's arrays. A program takes and returns all parts, laid end to end along the dimension named above; each array names one. Nothing has to cross between parts.
Inputs may be any that keep to these rules, and one draw needn't show every extreme that they name: `pair_count`: every tile has at least one active pair and some tile has 16. `pair_block`: the 16 slots of a tile name distinct blocks; slot 0 is the block of the tile's own tile row (block b belongs to tile row b); every slot's block b satisfies |b - floor(t / 16)| <= 16 for its tile t; slots at or beyond the tile's pair_count are ignored.
All inputs are finite; a program needn't handle non-finite values.
Results may differ from the reference program's by a relative error of at most 0.0003.
Values sent between devices are 32-bit elements; how exact they have to be, the bound alone decides.
No kernel may reach another device: no remote copies, remote signals or barrier semaphores. Data moves between devices by JAX's collectives and lax.ppermute only.
A program may use at most 64 MiB of HBM per device.

```python
import jax
import jax.numpy as jnp
from jax import lax

TSIDE = 16
CELLS = 256
FACS = 256
TILE_COLS = 16
KSLOTS = 16
ITERS = 2
REACH = 64
SPAN = 16
TILES = 256
BLOCKS = 16


def draw_facility_xy(key, part):
    key_x, key_y = jax.random.split(key, 2)
    row_ids = jnp.arange(BLOCKS, dtype=jnp.int32)[:, None].astype(jnp.float32)
    across = jax.random.uniform(key_x, (BLOCKS, FACS), jnp.float32) * (TILE_COLS * TSIDE)
    along = (row_ids + jax.random.uniform(key_y, (BLOCKS, FACS), jnp.float32)) * TSIDE
    return jnp.stack([across, along], axis=1)


def draw_pair_block(key, part):
    row_ids = jnp.arange(TILES, dtype=jnp.int32) // TILE_COLS
    offsets = jnp.arange(2 * SPAN + 1, dtype=jnp.int32) - SPAN
    candidate = row_ids[:, None] + offsets[None, :]
    inside = (candidate >= 0) & (candidate < BLOCKS)
    jitter = jax.random.randint(key, (TILES, 2 * SPAN + 1), 0, 96)
    ranking = jnp.abs(offsets)[None, :] * 64 + jitter
    ranking = jnp.where(offsets[None, :] == 0, -1, ranking)
    ranking = jnp.where(inside, ranking, 100000)
    ranking = ranking * 64 + offsets[None, :] + SPAN
    order = jnp.argsort(ranking, axis=1, stable=True)
    return jnp.take_along_axis(candidate, order[:, :KSLOTS], axis=1).astype(jnp.int32)


def draw_pair_count(key, part):
    key_level, key_count, key_pick = jax.random.split(key, 3)
    level = jax.random.randint(key_level, (TILES // TILE_COLS,), 0, 4)
    ceiling = 1 + level * level * (KSLOTS - 1) // 9
    per_tile = jnp.repeat(ceiling, TILE_COLS)
    counts = 1 + jax.random.randint(key_count, (TILES,), 0, per_tile)
    picked = jax.random.randint(key_pick, (), 0, TILES)
    counts = jnp.where(jnp.arange(TILES, dtype=jnp.int32) == picked, KSLOTS, counts)
    return counts.astype(jnp.int32)


def block_levels(own_key, dims, cuts, smallest, largest):
    loudness = 1.0
    for position, blocks in cuts:
        heights = jax.random.uniform(jax.random.fold_in(jax.random.fold_in(own_key, 6), position), (blocks,), jnp.float32, smallest / len(cuts), largest / len(cuts))
        loudness = loudness * jnp.repeat(jnp.exp(heights), dims[position] // blocks).reshape((-1,) + (1,) * (len(dims) - 1 - position))
    return loudness


def scatter_about(key, extent, spread, most, pieces=(), held_as=jnp.bfloat16):
    loudness = block_levels(key, extent, pieces, -0.22, 0.18) if pieces else 1.0
    values = jax.random.normal(key, extent, jnp.float32) * spread * loudness
    return jnp.minimum(jnp.maximum(values, -most), most).astype(held_as)


def setup_inputs(seed: int = 0, part: int = 0) -> dict:
    keys = jax.random.split(jax.random.key(seed), 7)
    part_keys = jax.random.split(jax.random.fold_in(keys[6], part), 7)
    return {
        "log_demand": jnp.clip(-3.0 + 3.0 * jax.random.uniform(part_keys[0], (TILES, CELLS), jnp.float32) ** block_levels(part_keys[0], (TILES, CELLS), ((0, 16),), -0.2, 0.2), -3.0, 0.0),
        "log_capacity": jnp.clip(jax.random.uniform(part_keys[1], (BLOCKS, FACS), jnp.float32, -1.0, 1.0) * block_levels(part_keys[1], (BLOCKS, FACS), ((0, 16),), -0.4, 0.0), -1.0, 1.0),
        "warm_potential": scatter_about(part_keys[2], (BLOCKS, FACS), 1.0, 4.0, ((0, 16),), jnp.float32),
        "facility_xy": draw_facility_xy(jax.random.fold_in(jax.random.fold_in(keys[6], part), 71), part),
        "pair_block": draw_pair_block(jax.random.fold_in(jax.random.fold_in(keys[6], part), 71), part),
        "pair_count": draw_pair_count(jax.random.fold_in(jax.random.fold_in(keys[6], part), 71), part),
    }


LOWEST = -1.0e30


def cell_coords(tile_index):
    cell_ids = jnp.arange(TSIDE * TSIDE, dtype=jnp.int32)
    column = (tile_index % TILE_COLS) * TSIDE + cell_ids % TSIDE
    row_cell = (tile_index // TILE_COLS) * TSIDE + cell_ids // TSIDE
    return column.astype(jnp.float32) + 0.5, row_cell.astype(jnp.float32) + 0.5


def pair_cost(coord_x, coord_y, positions):
    delta_x = coord_x[None, :, None] - positions[:, 0, :][:, None, :]
    delta_y = coord_y[None, :, None] - positions[:, 1, :][:, None, :]
    return (delta_x * delta_x + delta_y * delta_y) / float(REACH * REACH)


def tile_pass(tile_index, demand_row, potentials, positions, active):
    coord_x, coord_y = cell_coords(tile_index)
    pair_costs = pair_cost(coord_x, coord_y, positions)
    scores = jnp.where(active[:, None, None], potentials[:, None, :] - pair_costs, LOWEST)
    row_top = jnp.max(scores, axis=(0, 2))
    row_sum = jnp.sum(jnp.exp(scores - row_top[None, :, None]), axis=(0, 2))
    cell_pot = demand_row - (row_top + jnp.log(row_sum))
    column_scores = cell_pot[None, :, None] - pair_costs
    col_top = jnp.max(column_scores, axis=1)
    col_sum = jnp.sum(jnp.exp(column_scores - col_top[:, None, :]), axis=1)
    col_top = jnp.where(active[:, None], col_top, LOWEST)
    col_sum = jnp.where(active[:, None], col_sum, 0.0)
    return cell_pot, col_top, col_sum


def reference(log_demand, log_capacity, warm_potential, facility_xy, pair_block, pair_count):
    slot_ids = jnp.arange(KSLOTS, dtype=jnp.int32)
    facility_pot = warm_potential
    cell_pot = log_demand
    for step_index in range(ITERS):
        current = facility_pot

        def one_tile(tile_index):
            active = slot_ids < pair_count[tile_index]
            blocks = pair_block[tile_index]
            return tile_pass(tile_index, log_demand[tile_index], current[blocks], facility_xy[blocks], active)

        cell_pot, col_top, col_sum = lax.map(one_tile, jnp.arange(TILES, dtype=jnp.int32))
        flat_ids = pair_block.reshape(-1)
        flat_top = col_top.reshape(-1, FACS)
        flat_sum = col_sum.reshape(-1, FACS)
        block_top = jnp.full((BLOCKS, FACS), LOWEST, jnp.float32).at[flat_ids].max(flat_top)
        block_sum = jnp.zeros((BLOCKS, FACS), jnp.float32).at[flat_ids].add(flat_sum * jnp.exp(flat_top - block_top[flat_ids]))
        facility_pot = log_capacity - (block_top + jnp.log(block_sum))
    return cell_pot, facility_pot
```

```python
import jax
import jax.numpy as jnp
from jax import lax
from jax.experimental import pallas as pl
from jax.experimental.pallas import tpu as pltpu
from jax.sharding import PartitionSpec as P

TSIDE = 16
TILE_COLS = 16
KSLOTS = 16
ITERS = 2
REACH = 64
SPAN = 16


LOWEST = -1e30

HALF = TSIDE * TILE_COLS // 2
COLS_HALF = TILE_COLS // 2
SCALE = 1.0 / float(REACH * REACH)
MIDDLE = 736.0
ROW_POT = TSIDE
ROW_CAP = TSIDE + 2
ROW_MASK = TSIDE + 4
ROWS = TSIDE + 8


def dot_nt(a, b):
    return lax.dot_general(a, b, (((1,), (1,)), ((), ())), preferred_element_type=jnp.float32)


def dot_nn(a, b):
    return lax.dot_general(a, b, (((1,), (0,)), ((), ())), preferred_element_type=jnp.float32)


def split(values):
    high = values.astype(jnp.bfloat16)
    low = (values - high.astype(jnp.float32)).astype(jnp.bfloat16)
    return high, low


def center_cost(xy_ref, block, core, rows):
    fx = xy_ref[block, 0:1, :]
    fy = xy_ref[block, 1:2, :]
    x_mid = (core * HALF).astype(jnp.float32) + 0.5 * HALF
    y_mid = (lax.broadcasted_iota(jnp.int32, (rows, 1), 0) * TSIDE).astype(jnp.float32) + 0.5 * TSIDE
    dx = x_mid - fx
    dy = y_mid - fy
    return (dx * dx + dy * dy) * SCALE


def y_factor(xy_ref, block):
    offset = lax.broadcasted_iota(jnp.int32, (TSIDE, 1), 0).astype(jnp.float32) - 0.5 * (TSIDE - 1)
    return jnp.exp(offset * ((xy_ref[block, 1:2, :] - MIDDLE) * (2.0 * SCALE)))


def x_factor(xy_ref, block):
    offset = lax.broadcasted_iota(jnp.int32, (HALF, 1), 0).astype(jnp.float32) - 0.5 * (HALF - 1)
    return jnp.exp(offset * ((xy_ref[block, 0:1, :] - MIDDLE) * (2.0 * SCALE)))


def build_mask(recv_ref, mask_ref, rows, blocks):
    marks = recv_ref[:, ROW_MASK, :]
    lane_block = lax.broadcasted_iota(jnp.int32, (blocks, rows, HALF), 2) // COLS_HALF
    own_block = lax.broadcasted_iota(jnp.int32, (blocks, rows, HALF), 0)
    picked = jnp.where(lane_block == own_block, marks[None], 0.0)
    picked = picked.reshape(blocks * rows, HALF).astype(jnp.bfloat16)
    source = lax.broadcasted_iota(jnp.int32, (HALF, HALF), 0) % COLS_HALF
    target = lax.broadcasted_iota(jnp.int32, (HALF, HALF), 1) // TSIDE
    spread = jnp.where(source == target, 1.0, 0.0).astype(jnp.bfloat16)
    mask_ref[...] = dot_nn(picked, spread).reshape(blocks, rows, HALF)


def row_pass(recv_ref, xy_ref, pot_of, mask_ref, top_ref, xf_ref, acc_ref, core, rows, blocks):
    def tops(block, best):
        scores = pot_of(block) - center_cost(xy_ref, block, core, rows)
        top = jnp.broadcast_to(jnp.max(scores, axis=1, keepdims=True), (rows, HALF))
        top_ref[block] = top
        return jnp.maximum(best, jnp.where(mask_ref[block] > 0.0, top, LOWEST))

    best = lax.fori_loop(0, blocks, tops, jnp.full((rows, HALF), LOWEST, jnp.float32))
    acc_ref[...] = jnp.zeros_like(acc_ref)

    def sums(block, carry):
        high, low = split(x_factor(xy_ref, block))
        xf_ref[block, :HALF, :] = high
        xf_ref[block, HALF:, :] = low
        top = top_ref[block]
        scores = pot_of(block) - center_cost(xy_ref, block, core, rows)
        weight = jnp.exp(scores - top[:, 0:1])
        lhs = weight[:, None, :] * y_factor(xy_ref, block)[None]
        a_high, a_low = split(lhs.reshape(rows * TSIDE, lhs.shape[-1]))
        both = dot_nt(a_high, xf_ref[block])
        third = dot_nt(a_low, xf_ref[block, :HALF, :])
        part = both[:, :HALF] + both[:, HALF:] + third
        scale = jnp.where(mask_ref[block] > 0.0, jnp.exp(jnp.minimum(top - best, 0.0)), 0.0)
        acc_ref[...] += part.reshape(rows, TSIDE, HALF) * scale[:, None, :]
        return carry

    lax.fori_loop(0, blocks, sums, 0)
    demand = recv_ref[:, :TSIDE, :]
    return demand - best[:, None, :] - jnp.log(acc_ref[...])


def column_part(xy_ref, mask_ref, xf_ref, level, base, block, core, rows):
    active = mask_ref[block] > 0.0
    top = jnp.max(jnp.where(active, level, LOWEST), axis=1, keepdims=True)
    scale = jnp.where(active, jnp.exp(jnp.minimum(level - top, 0.0)), 0.0)
    weights = (base * scale[:, None, :]).reshape(rows * TSIDE, HALF)
    w_high, w_low = split(weights)
    mixed = dot_nn(jnp.concatenate([w_high, w_high], axis=1), xf_ref[block])
    mixed = mixed + dot_nn(w_low, xf_ref[block, :HALF, :])
    width = mixed.shape[-1]
    sums = jnp.sum(mixed.reshape(rows, TSIDE, width) * y_factor(xy_ref, block)[None], axis=1)
    tops = top - center_cost(xy_ref, block, core, rows)
    best = jnp.max(tops, axis=0, keepdims=True)
    total = jnp.sum(sums * jnp.exp(tops - best), axis=0, keepdims=True)
    return best + jnp.log(total)


def first_kernel(rows, blocks, recv_ref, xy_ref, part_ref, mask_ref, top_ref, xf_ref, acc_ref):
    core = lax.axis_index("tile") % 2
    build_mask(recv_ref, mask_ref, rows, blocks)

    def pot_of(block):
        return jnp.concatenate(
            [recv_ref[block, ROW_POT : ROW_POT + 1, :], recv_ref[block, ROW_POT + 1 : ROW_POT + 2, :]], axis=1
        )

    shifted = row_pass(recv_ref, xy_ref, pot_of, mask_ref, top_ref, xf_ref, acc_ref, core, rows, blocks)
    level = jnp.max(shifted, axis=1)
    acc_ref[...] = jnp.exp(shifted - level[:, None, :])

    def columns(block, carry):
        part_ref[pl.ds(block, 1), :] = column_part(
            xy_ref, mask_ref, xf_ref, level, acc_ref[...], block, core, rows
        )
        return carry

    lax.fori_loop(0, blocks, columns, 0)


def log_add(a, b):
    top = jnp.maximum(a, b)
    return top + jnp.log(jnp.exp(a - top) + jnp.exp(b - top))


def second_kernel(
    rows, blocks, recv_ref, xy_ref, mine_ref, other_ref, keep_ref, send_ref, pot_ref, mask_ref, top_ref, xf_ref, acc_ref
):
    me = lax.axis_index("tile")
    core = me % 2
    build_mask(recv_ref, mask_ref, rows, blocks)
    capacity = jnp.concatenate([recv_ref[:, ROW_CAP, :], recv_ref[:, ROW_CAP + 1, :]], axis=1)
    pot_ref[...] = capacity - log_add(mine_ref[...], other_ref[...])

    def pot_of(block):
        return pot_ref[pl.ds(block, 1), :]

    shifted = row_pass(recv_ref, xy_ref, pot_of, mask_ref, top_ref, xf_ref, acc_ref, core, rows, blocks)
    level = jnp.max(shifted, axis=1)
    acc_ref[...] = shifted
    x_mid = (core * HALF).astype(jnp.float32) + 0.5 * HALF
    dx = lax.broadcasted_iota(jnp.int32, (1, HALF), 1).astype(jnp.float32) - 0.5 * (HALF - 1)
    dy = lax.broadcasted_iota(jnp.int32, (TSIDE, 1), 0).astype(jnp.float32) - 0.5 * (TSIDE - 1)
    for row, out_ref in ((me, keep_ref), (me + 1 - 2 * core, send_ref)):
        y_mid = (row * TSIDE).astype(jnp.float32) + 0.5 * TSIDE
        lift = (dx * (dx + 2.0 * (x_mid - MIDDLE)) + dy * (dy + 2.0 * (y_mid - MIDDLE))) * SCALE
        out_ref[:TSIDE, :] = acc_ref[row] + lift
        part = column_part(
            xy_ref, mask_ref, xf_ref, level, jnp.exp(shifted - level[:, None, :]), row, core, rows
        )
        out_ref[ROW_POT : ROW_POT + 1, :] = part[:, :HALF]
        out_ref[ROW_POT + 1 : ROW_POT + 2, :] = part[:, HALF:]
        out_ref[ROW_POT + 2 :, :] = jnp.zeros((ROWS - ROW_POT - 2, HALF), jnp.float32)


def on_device_all_rows(log_demand, log_capacity, warm_potential, facility_xy, pair_block, pair_count):
    devices = lax.axis_size("tile")
    me = lax.axis_index("tile")
    rows = devices
    blocks = facility_xy.shape[0]
    width = log_capacity.shape[1]
    demand = log_demand.reshape(TILE_COLS, TSIDE, TSIDE).transpose(1, 0, 2).reshape(TSIDE, 2, HALF)
    active = jnp.arange(KSLOTS, dtype=jnp.int32)[None, :] < pair_count[:, None]
    block_ids = jnp.arange(blocks, dtype=jnp.int32)
    hits = (pair_block[None] == block_ids[:, None, None]) & active[None]
    marks = jnp.max(hits.astype(jnp.float32), axis=2)
    marks = marks.reshape(blocks, 2, COLS_HALF).transpose(1, 0, 2).reshape(2, 1, HALF)
    small = jnp.concatenate([warm_potential.reshape(2, HALF), log_capacity.reshape(2, HALF)], axis=0)
    small = jnp.broadcast_to(small[None], (2, 4, HALF))
    message = jnp.concatenate(
        [demand.transpose(1, 0, 2), small, marks, jnp.zeros((2, ROWS - ROW_MASK - 1, HALF), jnp.float32)], axis=1
    )
    message = jnp.broadcast_to(message[None], (devices // 2, 2, ROWS, HALF)).reshape(devices, ROWS, HALF)
    recv = lax.all_to_all(message, "tile", 0, 0, tiled=True)
    scratch = [
        pltpu.VMEM((blocks, rows, HALF), jnp.float32),
        pltpu.VMEM((blocks, rows, HALF), jnp.float32),
        pltpu.VMEM((blocks, 2 * HALF, width), jnp.bfloat16),
        pltpu.VMEM((rows, TSIDE, HALF), jnp.float32),
    ]
    params = pltpu.CompilerParams(vmem_limit_bytes=48 * 1024 * 1024)
    part = pl.pallas_call(
        lambda *refs: first_kernel(rows, blocks, *refs),
        out_shape=jax.ShapeDtypeStruct((blocks, width), jnp.float32),
        scratch_shapes=scratch,
        compiler_params=params,
        name="first_iteration",
    )(recv, facility_xy)
    swap = [(i, i ^ 1) for i in range(devices)]
    other = lax.ppermute(part, "tile", swap)
    keep, send = pl.pallas_call(
        lambda *refs: second_kernel(rows, blocks, *refs),
        out_shape=(
            jax.ShapeDtypeStruct((ROWS, HALF), jnp.float32),
            jax.ShapeDtypeStruct((ROWS, HALF), jnp.float32),
        ),
        scratch_shapes=[pltpu.VMEM((blocks, width), jnp.float32)] + scratch,
        compiler_params=params,
        name="second_iteration",
    )(recv, facility_xy, part, other)
    got = lax.ppermute(send, "tile", swap)
    is_left = me % 2 == 0
    left = jnp.where(is_left, keep, got)
    right = jnp.where(is_left, got, keep)
    cells = jnp.concatenate([left[:TSIDE], right[:TSIDE]], axis=1)
    cell_pot = cells.reshape(TSIDE, TILE_COLS, TSIDE).transpose(1, 0, 2).reshape(TILE_COLS, TSIDE * TSIDE)
    total = log_add(keep[ROW_POT : ROW_POT + 2], got[ROW_POT : ROW_POT + 2])
    facility_pot = log_capacity - total.reshape(1, width)
    return (cell_pot, facility_pot)


def from_behind(block, axis, distance):
    devices = range(lax.axis_size(axis))
    route = [(i - distance, i) for i in devices if i - distance in devices]
    return lax.ppermute(block, axis, route)


def cell_coords(tile_index):
    cell_ids = jnp.arange(TSIDE * TSIDE, dtype=jnp.int32)
    column = tile_index % TILE_COLS * TSIDE + cell_ids % TSIDE
    row_cell = tile_index // TILE_COLS * TSIDE + cell_ids // TSIDE
    return (column.astype(jnp.float32) + 0.5, row_cell.astype(jnp.float32) + 0.5)


def pair_cost(coord_x, coord_y, positions):
    delta_x = coord_x[None, :, None] - positions[:, 0, :][:, None, :]
    delta_y = coord_y[None, :, None] - positions[:, 1, :][:, None, :]
    return (delta_x * delta_x + delta_y * delta_y) / float(REACH * REACH)


def tile_pass(tile_index, demand_row, potentials, positions, active):
    coord_x, coord_y = cell_coords(tile_index)
    pair_costs = pair_cost(coord_x, coord_y, positions)
    scores = jnp.where(active[:, None, None], potentials[:, None, :] - pair_costs, LOWEST)
    row_top = jnp.max(scores, axis=(0, 2))
    row_sum = jnp.sum(jnp.exp(scores - row_top[None, :, None]), axis=(0, 2))
    cell_pot = demand_row - (row_top + jnp.log(row_sum))
    column_scores = cell_pot[None, :, None] - pair_costs
    col_top = jnp.max(column_scores, axis=1)
    col_sum = jnp.sum(jnp.exp(column_scores - col_top[:, None, :]), axis=1)
    col_top = jnp.where(active[:, None], col_top, LOWEST)
    col_sum = jnp.where(active[:, None], col_sum, 0.0)
    return (cell_pot, col_top, col_sum)


def merge_parts(top_a, sum_a, top_b, sum_b):
    top_new = jnp.maximum(top_a, top_b)
    return (top_new, sum_a * jnp.exp(top_a - top_new) + sum_b * jnp.exp(top_b - top_new))


def on_device(log_demand, log_capacity, warm_potential, facility_xy, pair_block, pair_count):
    tiles_here = log_demand.shape[0]
    blocks_here = log_capacity.shape[0]
    block_width = log_capacity.shape[1]
    devices_along = lax.axis_size("tile")
    my_index = lax.axis_index("tile")
    reach = min(devices_along - 1, (SPAN + blocks_here - 1) // blocks_here)
    window = 2 * reach + 1
    tile_ids = my_index * tiles_here + jnp.arange(tiles_here, dtype=jnp.int32)
    slot_ids = jnp.arange(KSLOTS, dtype=jnp.int32)
    first_block = (my_index - reach) * blocks_here
    local_block = pair_block - first_block
    facility_pot = warm_potential
    cell_pot = log_demand
    for step_index in range(ITERS):
        slabs = []
        for position in range(window):
            distance = reach - position
            if distance == 0:
                slabs.append(facility_pot)
            else:
                slabs.append(from_behind(facility_pot, "tile", distance))
        window_pot = jnp.concatenate(slabs, axis=0)

        def one_tile(inputs):
            tile_index, demand_row, blocks, nearby, slot_limit = inputs
            active = slot_ids < slot_limit
            return tile_pass(
                tile_index, demand_row, window_pot[nearby], facility_xy[blocks], active
            )

        cell_pot, col_top, col_sum = lax.map(
            one_tile, (tile_ids, log_demand, pair_block, local_block, pair_count)
        )
        flat_ids = local_block.reshape(-1)
        flat_top = col_top.reshape(-1, block_width)
        flat_sum = col_sum.reshape(-1, block_width)
        local_top = (
            jnp.full((window * blocks_here, block_width), LOWEST, jnp.float32)
            .at[flat_ids]
            .max(flat_top)
        )
        local_sum = (
            jnp.zeros((window * blocks_here, block_width), jnp.float32)
            .at[flat_ids]
            .add(flat_sum * jnp.exp(flat_top - local_top[flat_ids]))
        )

        def slab_of(position):
            return (
                local_top[position * blocks_here : (position + 1) * blocks_here],
                local_sum[position * blocks_here : (position + 1) * blocks_here],
            )

        own_top, block_sum = slab_of(reach)
        for distance in range(-reach, reach + 1):
            if distance != 0:
                send_top, send_sum = slab_of(reach + distance)
                got_top, got_sum = from_behind((send_top, send_sum), "tile", distance)
                source = my_index - distance
                valid = (source >= 0) & (source < devices_along)
                got_top = jnp.where(valid, got_top, LOWEST)
                got_sum = jnp.where(valid, got_sum, 0.0)
                own_top, block_sum = merge_parts(own_top, block_sum, got_top, got_sum)
        facility_pot = log_capacity - (own_top + jnp.log(block_sum))
    return (cell_pot, facility_pot)


def solution(mesh):
    placed = (
        P(("groups", "tile"), None),
        P(("groups", "tile"), None),
        P(("groups", "tile"), None),
        P("groups", None, None),
        P(("groups", "tile"), None),
        P(("groups", "tile")),
    )
    devices = mesh.shape["tile"]
    small = devices % 2 == 0 and devices * COLS_HALF == HALF

    def program(log_demand, log_capacity, warm_potential, facility_xy, pair_block, pair_count):
        one_row = log_demand.shape[0] == mesh.size * TILE_COLS and log_capacity.shape[0] == mesh.size
        fits = small and one_row and log_capacity.shape[1] == 2 * HALF
        body = on_device_all_rows if fits else on_device
        return jax.shard_map(
            body,
            mesh=mesh,
            in_specs=placed,
            out_specs=(P(("groups", "tile"), None), P(("groups", "tile"), None)),
            check_vma=False,
        )(log_demand, log_capacity, warm_potential, facility_xy, pair_block, pair_count)

    return program
```

```python
import jax
import jax.numpy as jnp
from jax import lax
from jax.experimental import pallas as pl
from jax.experimental.pallas import tpu as pltpu
from jax.sharding import PartitionSpec as P

TSIDE = 16
TILE_COLS = 16
KSLOTS = 16
ITERS = 2
REACH = 64
SPAN = 16


LOWEST = -1e30

HALF = TSIDE * TILE_COLS // 2
COLS_HALF = TILE_COLS // 2
SCALE = 1.0 / float(REACH * REACH)
MIDDLE = 736.0
ROW_POT = TSIDE
ROW_CAP = TSIDE + 2
ROW_MASK = TSIDE + 4
ROWS = TSIDE + 8


def dot_nt(a, b):
    return lax.dot_general(a, b, (((1,), (1,)), ((), ())), preferred_element_type=jnp.float32)


def dot_nn(a, b):
    return lax.dot_general(a, b, (((1,), (0,)), ((), ())), preferred_element_type=jnp.float32)


def split(values):
    high = values.astype(jnp.bfloat16)
    low = (values - high.astype(jnp.float32)).astype(jnp.bfloat16)
    return high, low


def center_cost(xy_ref, block, core, rows):
    fx = xy_ref[block, 0:1, :]
    fy = xy_ref[block, 1:2, :]
    x_mid = (core * HALF).astype(jnp.float32) + 0.5 * HALF
    y_mid = (lax.broadcasted_iota(jnp.int32, (rows, 1), 0) * TSIDE).astype(jnp.float32) + 0.5 * TSIDE
    dx = x_mid - fx
    dy = y_mid - fy
    return (dx * dx + dy * dy) * SCALE


def y_factor(xy_ref, block):
    offset = lax.broadcasted_iota(jnp.int32, (TSIDE, 1), 0).astype(jnp.float32) - 0.5 * (TSIDE - 1)
    return jnp.exp(offset * ((xy_ref[block, 1:2, :] - MIDDLE) * (2.0 * SCALE)))


def x_factor(xy_ref, block):
    offset = lax.broadcasted_iota(jnp.int32, (HALF, 1), 0).astype(jnp.float32) - 0.5 * (HALF - 1)
    return jnp.exp(offset * ((xy_ref[block, 0:1, :] - MIDDLE) * (2.0 * SCALE)))


def build_mask(recv_ref, mask_ref, rows, blocks):
    marks = recv_ref[:, ROW_MASK, :]
    lane_block = lax.broadcasted_iota(jnp.int32, (blocks, rows, HALF), 2) // COLS_HALF
    own_block = lax.broadcasted_iota(jnp.int32, (blocks, rows, HALF), 0)
    picked = jnp.where(lane_block == own_block, marks[None], 0.0)
    picked = picked.reshape(blocks * rows, HALF).astype(jnp.bfloat16)
    source = lax.broadcasted_iota(jnp.int32, (HALF, HALF), 0) % COLS_HALF
    target = lax.broadcasted_iota(jnp.int32, (HALF, HALF), 1) // TSIDE
    spread = jnp.where(source == target, 1.0, 0.0).astype(jnp.bfloat16)
    mask_ref[...] = dot_nn(picked, spread).reshape(blocks, rows, HALF)


def row_pass(recv_ref, xy_ref, pot_of, mask_ref, top_ref, xf_ref, acc_ref, core, rows, blocks):
    def tops(block, best):
        scores = pot_of(block) - center_cost(xy_ref, block, core, rows)
        top = jnp.broadcast_to(jnp.max(scores, axis=1, keepdims=True), (rows, HALF))
        top_ref[block] = top
        return jnp.maximum(best, jnp.where(mask_ref[block] > 0.0, top, LOWEST))

    best = lax.fori_loop(0, blocks, tops, jnp.full((rows, HALF), LOWEST, jnp.float32), unroll=True)
    acc_ref[...] = jnp.zeros_like(acc_ref)

    def sums(block, carry):
        high, low = split(x_factor(xy_ref, block))
        xf_ref[block, :HALF, :] = high
        xf_ref[block, HALF:, :] = low
        top = top_ref[block]
        scores = pot_of(block) - center_cost(xy_ref, block, core, rows)
        weight = jnp.exp(scores - top[:, 0:1])
        lhs = weight[:, None, :] * y_factor(xy_ref, block)[None]
        a_high, a_low = split(lhs.reshape(rows * TSIDE, lhs.shape[-1]))
        both = dot_nt(a_high, xf_ref[block])
        third = dot_nt(a_low, xf_ref[block, :HALF, :])
        part = both[:, :HALF] + both[:, HALF:] + third
        scale = jnp.where(mask_ref[block] > 0.0, jnp.exp(jnp.minimum(top - best, 0.0)), 0.0)
        acc_ref[...] += part.reshape(rows, TSIDE, HALF) * scale[:, None, :]
        return carry

    lax.fori_loop(0, blocks, sums, 0, unroll=True)
    demand = recv_ref[:, :TSIDE, :]
    return demand - best[:, None, :] - jnp.log(acc_ref[...])


def column_part(xy_ref, mask_ref, xf_ref, level, base, block, core, rows):
    active = mask_ref[block] > 0.0
    top = jnp.max(jnp.where(active, level, LOWEST), axis=1, keepdims=True)
    scale = jnp.where(active, jnp.exp(jnp.minimum(level - top, 0.0)), 0.0)
    weights = (base * scale[:, None, :]).reshape(rows * TSIDE, HALF)
    w_high, w_low = split(weights)
    mixed = dot_nn(jnp.concatenate([w_high, w_high], axis=1), xf_ref[block])
    mixed = mixed + dot_nn(w_low, xf_ref[block, :HALF, :])
    width = mixed.shape[-1]
    sums = jnp.sum(mixed.reshape(rows, TSIDE, width) * y_factor(xy_ref, block)[None], axis=1)
    tops = top - center_cost(xy_ref, block, core, rows)
    best = jnp.max(tops, axis=0, keepdims=True)
    total = jnp.sum(sums * jnp.exp(tops - best), axis=0, keepdims=True)
    return best + jnp.log(total)


def first_kernel(rows, blocks, recv_ref, xy_ref, part_ref, mask_ref, top_ref, xf_ref, acc_ref):
    core = lax.axis_index("tile") % 2
    build_mask(recv_ref, mask_ref, rows, blocks)

    def pot_of(block):
        return jnp.concatenate(
            [recv_ref[block, ROW_POT : ROW_POT + 1, :], recv_ref[block, ROW_POT + 1 : ROW_POT + 2, :]], axis=1
        )

    shifted = row_pass(recv_ref, xy_ref, pot_of, mask_ref, top_ref, xf_ref, acc_ref, core, rows, blocks)
    level = jnp.max(shifted, axis=1)
    acc_ref[...] = jnp.exp(shifted - level[:, None, :])

    def columns(block, carry):
        part_ref[pl.ds(block, 1), :] = column_part(
            xy_ref, mask_ref, xf_ref, level, acc_ref[...], block, core, rows
        )
        return carry

    lax.fori_loop(0, blocks, columns, 0, unroll=True)


def log_add(a, b):
    top = jnp.maximum(a, b)
    return top + jnp.log(jnp.exp(a - top) + jnp.exp(b - top))


def second_kernel(
    rows, blocks, recv_ref, xy_ref, mine_ref, other_ref, keep_ref, send_ref, pot_ref, mask_ref, top_ref, xf_ref, acc_ref
):
    me = lax.axis_index("tile")
    core = me % 2
    build_mask(recv_ref, mask_ref, rows, blocks)
    capacity = jnp.concatenate([recv_ref[:, ROW_CAP, :], recv_ref[:, ROW_CAP + 1, :]], axis=1)
    pot_ref[...] = capacity - log_add(mine_ref[...], other_ref[...])

    def pot_of(block):
        return pot_ref[pl.ds(block, 1), :]

    shifted = row_pass(recv_ref, xy_ref, pot_of, mask_ref, top_ref, xf_ref, acc_ref, core, rows, blocks)
    level = jnp.max(shifted, axis=1)
    acc_ref[...] = shifted
    x_mid = (core * HALF).astype(jnp.float32) + 0.5 * HALF
    dx = lax.broadcasted_iota(jnp.int32, (1, HALF), 1).astype(jnp.float32) - 0.5 * (HALF - 1)
    dy = lax.broadcasted_iota(jnp.int32, (TSIDE, 1), 0).astype(jnp.float32) - 0.5 * (TSIDE - 1)
    for row, out_ref in ((me, keep_ref), (me + 1 - 2 * core, send_ref)):
        y_mid = (row * TSIDE).astype(jnp.float32) + 0.5 * TSIDE
        lift = (dx * (dx + 2.0 * (x_mid - MIDDLE)) + dy * (dy + 2.0 * (y_mid - MIDDLE))) * SCALE
        out_ref[:TSIDE, :] = acc_ref[row] + lift
        part = column_part(
            xy_ref, mask_ref, xf_ref, level, jnp.exp(shifted - level[:, None, :]), row, core, rows
        )
        out_ref[ROW_POT : ROW_POT + 1, :] = part[:, :HALF]
        out_ref[ROW_POT + 1 : ROW_POT + 2, :] = part[:, HALF:]
        out_ref[ROW_POT + 2 :, :] = jnp.zeros((ROWS - ROW_POT - 2, HALF), jnp.float32)


def on_device_all_rows(log_demand, log_capacity, warm_potential, facility_xy, pair_block, pair_count):
    devices = lax.axis_size("tile")
    me = lax.axis_index("tile")
    rows = devices
    blocks = facility_xy.shape[0]
    width = log_capacity.shape[1]
    demand = log_demand.reshape(TILE_COLS, TSIDE, TSIDE).transpose(1, 0, 2).reshape(TSIDE, 2, HALF)
    active = jnp.arange(KSLOTS, dtype=jnp.int32)[None, :] < pair_count[:, None]
    block_ids = jnp.arange(blocks, dtype=jnp.int32)
    hits = (pair_block[None] == block_ids[:, None, None]) & active[None]
    marks = jnp.max(hits.astype(jnp.float32), axis=2)
    marks = marks.reshape(blocks, 2, COLS_HALF).transpose(1, 0, 2).reshape(2, 1, HALF)
    small = jnp.concatenate([warm_potential.reshape(2, HALF), log_capacity.reshape(2, HALF)], axis=0)
    small = jnp.broadcast_to(small[None], (2, 4, HALF))
    message = jnp.concatenate(
        [demand.transpose(1, 0, 2), small, marks, jnp.zeros((2, ROWS - ROW_MASK - 1, HALF), jnp.float32)], axis=1
    )
    message = jnp.broadcast_to(message[None], (devices // 2, 2, ROWS, HALF)).reshape(devices, ROWS, HALF)
    recv = lax.all_to_all(message, "tile", 0, 0, tiled=True)
    scratch = [
        pltpu.VMEM((blocks, rows, HALF), jnp.float32),
        pltpu.VMEM((blocks, rows, HALF), jnp.float32),
        pltpu.VMEM((blocks, 2 * HALF, width), jnp.bfloat16),
        pltpu.VMEM((rows, TSIDE, HALF), jnp.float32),
    ]
    params = pltpu.CompilerParams(vmem_limit_bytes=48 * 1024 * 1024)
    part = pl.pallas_call(
        lambda *refs: first_kernel(rows, blocks, *refs),
        out_shape=jax.ShapeDtypeStruct((blocks, width), jnp.float32),
        scratch_shapes=scratch,
        compiler_params=params,
        name="first_iteration",
    )(recv, facility_xy)
    swap = [(i, i ^ 1) for i in range(devices)]
    other = lax.ppermute(part, "tile", swap)
    keep, send = pl.pallas_call(
        lambda *refs: second_kernel(rows, blocks, *refs),
        out_shape=(
            jax.ShapeDtypeStruct((ROWS, HALF), jnp.float32),
            jax.ShapeDtypeStruct((ROWS, HALF), jnp.float32),
        ),
        scratch_shapes=[pltpu.VMEM((blocks, width), jnp.float32)] + scratch,
        compiler_params=params,
        name="second_iteration",
    )(recv, facility_xy, part, other)
    got = lax.ppermute(send, "tile", swap)
    is_left = me % 2 == 0
    left = jnp.where(is_left, keep, got)
    right = jnp.where(is_left, got, keep)
    cells = jnp.concatenate([left[:TSIDE], right[:TSIDE]], axis=1)
    cell_pot = cells.reshape(TSIDE, TILE_COLS, TSIDE).transpose(1, 0, 2).reshape(TILE_COLS, TSIDE * TSIDE)
    total = log_add(keep[ROW_POT : ROW_POT + 2], got[ROW_POT : ROW_POT + 2])
    facility_pot = log_capacity - total.reshape(1, width)
    return (cell_pot, facility_pot)


def from_behind(block, axis, distance):
    devices = range(lax.axis_size(axis))
    route = [(i - distance, i) for i in devices if i - distance in devices]
    return lax.ppermute(block, axis, route)


def cell_coords(tile_index):
    cell_ids = jnp.arange(TSIDE * TSIDE, dtype=jnp.int32)
    column = tile_index % TILE_COLS * TSIDE + cell_ids % TSIDE
    row_cell = tile_index // TILE_COLS * TSIDE + cell_ids // TSIDE
    return (column.astype(jnp.float32) + 0.5, row_cell.astype(jnp.float32) + 0.5)


def pair_cost(coord_x, coord_y, positions):
    delta_x = coord_x[None, :, None] - positions[:, 0, :][:, None, :]
    delta_y = coord_y[None, :, None] - positions[:, 1, :][:, None, :]
    return (delta_x * delta_x + delta_y * delta_y) / float(REACH * REACH)


def tile_pass(tile_index, demand_row, potentials, positions, active):
    coord_x, coord_y = cell_coords(tile_index)
    pair_costs = pair_cost(coord_x, coord_y, positions)
    scores = jnp.where(active[:, None, None], potentials[:, None, :] - pair_costs, LOWEST)
    row_top = jnp.max(scores, axis=(0, 2))
    row_sum = jnp.sum(jnp.exp(scores - row_top[None, :, None]), axis=(0, 2))
    cell_pot = demand_row - (row_top + jnp.log(row_sum))
    column_scores = cell_pot[None, :, None] - pair_costs
    col_top = jnp.max(column_scores, axis=1)
    col_sum = jnp.sum(jnp.exp(column_scores - col_top[:, None, :]), axis=1)
    col_top = jnp.where(active[:, None], col_top, LOWEST)
    col_sum = jnp.where(active[:, None], col_sum, 0.0)
    return (cell_pot, col_top, col_sum)


def merge_parts(top_a, sum_a, top_b, sum_b):
    top_new = jnp.maximum(top_a, top_b)
    return (top_new, sum_a * jnp.exp(top_a - top_new) + sum_b * jnp.exp(top_b - top_new))


def on_device(log_demand, log_capacity, warm_potential, facility_xy, pair_block, pair_count):
    tiles_here = log_demand.shape[0]
    blocks_here = log_capacity.shape[0]
    block_width = log_capacity.shape[1]
    devices_along = lax.axis_size("tile")
    my_index = lax.axis_index("tile")
    reach = min(devices_along - 1, (SPAN + blocks_here - 1) // blocks_here)
    window = 2 * reach + 1
    tile_ids = my_index * tiles_here + jnp.arange(tiles_here, dtype=jnp.int32)
    slot_ids = jnp.arange(KSLOTS, dtype=jnp.int32)
    first_block = (my_index - reach) * blocks_here
    local_block = pair_block - first_block
    facility_pot = warm_potential
    cell_pot = log_demand
    for step_index in range(ITERS):
        slabs = []
        for position in range(window):
            distance = reach - position
            if distance == 0:
                slabs.append(facility_pot)
            else:
                slabs.append(from_behind(facility_pot, "tile", distance))
        window_pot = jnp.concatenate(slabs, axis=0)

        def one_tile(inputs):
            tile_index, demand_row, blocks, nearby, slot_limit = inputs
            active = slot_ids < slot_limit
            return tile_pass(
                tile_index, demand_row, window_pot[nearby], facility_xy[blocks], active
            )

        cell_pot, col_top, col_sum = lax.map(
            one_tile, (tile_ids, log_demand, pair_block, local_block, pair_count)
        )
        flat_ids = local_block.reshape(-1)
        flat_top = col_top.reshape(-1, block_width)
        flat_sum = col_sum.reshape(-1, block_width)
        local_top = (
            jnp.full((window * blocks_here, block_width), LOWEST, jnp.float32)
            .at[flat_ids]
            .max(flat_top)
        )
        local_sum = (
            jnp.zeros((window * blocks_here, block_width), jnp.float32)
            .at[flat_ids]
            .add(flat_sum * jnp.exp(flat_top - local_top[flat_ids]))
        )

        def slab_of(position):
            return (
                local_top[position * blocks_here : (position + 1) * blocks_here],
                local_sum[position * blocks_here : (position + 1) * blocks_here],
            )

        own_top, block_sum = slab_of(reach)
        for distance in range(-reach, reach + 1):
            if distance != 0:
                send_top, send_sum = slab_of(reach + distance)
                got_top, got_sum = from_behind((send_top, send_sum), "tile", distance)
                source = my_index - distance
                valid = (source >= 0) & (source < devices_along)
                got_top = jnp.where(valid, got_top, LOWEST)
                got_sum = jnp.where(valid, got_sum, 0.0)
                own_top, block_sum = merge_parts(own_top, block_sum, got_top, got_sum)
        facility_pot = log_capacity - (own_top + jnp.log(block_sum))
    return (cell_pot, facility_pot)


def solution(mesh):
    placed = (
        P(("groups", "tile"), None),
        P(("groups", "tile"), None),
        P(("groups", "tile"), None),
        P("groups", None, None),
        P(("groups", "tile"), None),
        P(("groups", "tile")),
    )
    devices = mesh.shape["tile"]
    small = devices % 2 == 0 and devices * COLS_HALF == HALF

    def program(log_demand, log_capacity, warm_potential, facility_xy, pair_block, pair_count):
        one_row = log_demand.shape[0] == mesh.size * TILE_COLS and log_capacity.shape[0] == mesh.size
        fits = small and one_row and log_capacity.shape[1] == 2 * HALF
        body = on_device_all_rows if fits else on_device
        return jax.shard_map(
            body,
            mesh=mesh,
            in_specs=placed,
            out_specs=(P(("groups", "tile"), None), P(("groups", "tile"), None)),
            check_vma=False,
        )(log_demand, log_capacity, warm_potential, facility_xy, pair_block, pair_count)

    return program
```

```python
import jax
import jax.numpy as jnp
from jax import lax
from jax.experimental import pallas as pl
from jax.experimental.pallas import tpu as pltpu
from jax.sharding import PartitionSpec as P

TSIDE = 16
TILE_COLS = 16
KSLOTS = 16
ITERS = 2
REACH = 64
SPAN = 16


LOWEST = -1e30

HALF = TSIDE * TILE_COLS // 2
COLS_HALF = TILE_COLS // 2
SCALE = 1.0 / float(REACH * REACH)
MIDDLE = 736.0
ROW_POT = TSIDE
ROW_CAP = TSIDE + 2
ROW_MASK = TSIDE + 4
ROWS = TSIDE + 8


def dot_nt(a, b):
    return lax.dot_general(a, b, (((1,), (1,)), ((), ())), preferred_element_type=jnp.float32)


def dot_nn(a, b):
    return lax.dot_general(a, b, (((1,), (0,)), ((), ())), preferred_element_type=jnp.float32)


def split(values):
    high = values.astype(jnp.bfloat16)
    low = (values - high.astype(jnp.float32)).astype(jnp.bfloat16)
    return high, low


def center_cost(xy_ref, block, core, rows):
    fx = xy_ref[block, 0:1, :]
    fy = xy_ref[block, 1:2, :]
    x_mid = (core * HALF).astype(jnp.float32) + 0.5 * HALF
    y_mid = (lax.broadcasted_iota(jnp.int32, (rows, 1), 0) * TSIDE).astype(jnp.float32) + 0.5 * TSIDE
    dx = x_mid - fx
    dy = y_mid - fy
    return (dx * dx + dy * dy) * SCALE


def y_factor(xy_ref, block):
    offset = lax.broadcasted_iota(jnp.int32, (TSIDE, 1), 0).astype(jnp.float32) - 0.5 * (TSIDE - 1)
    return jnp.exp(offset * ((xy_ref[block, 1:2, :] - MIDDLE) * (2.0 * SCALE)))


def x_factor(xy_ref, block):
    offset = lax.broadcasted_iota(jnp.int32, (HALF, 1), 0).astype(jnp.float32) - 0.5 * (HALF - 1)
    return jnp.exp(offset * ((xy_ref[block, 0:1, :] - MIDDLE) * (2.0 * SCALE)))


def build_mask(recv_ref, mask_ref, rows, blocks):
    marks = recv_ref[:, ROW_MASK, :]
    lane_block = lax.broadcasted_iota(jnp.int32, (blocks, rows, HALF), 2) // COLS_HALF
    own_block = lax.broadcasted_iota(jnp.int32, (blocks, rows, HALF), 0)
    picked = jnp.where(lane_block == own_block, marks[None], 0.0)
    picked = picked.reshape(blocks * rows, HALF).astype(jnp.bfloat16)
    source = lax.broadcasted_iota(jnp.int32, (HALF, HALF), 0) % COLS_HALF
    target = lax.broadcasted_iota(jnp.int32, (HALF, HALF), 1) // TSIDE
    spread = jnp.where(source == target, 1.0, 0.0).astype(jnp.bfloat16)
    mask_ref[...] = dot_nn(picked, spread).reshape(blocks, rows, HALF)


def row_pass(recv_ref, xy_ref, pot_of, mask_ref, top_ref, xf_ref, acc_ref, core, rows, blocks):
    def tops(block, best):
        scores = pot_of(block) - center_cost(xy_ref, block, core, rows)
        top = jnp.broadcast_to(jnp.max(scores, axis=1, keepdims=True), (rows, HALF))
        top_ref[block] = top
        return jnp.maximum(best, jnp.where(mask_ref[block] > 0.0, top, LOWEST))

    best = lax.fori_loop(0, blocks, tops, jnp.full((rows, HALF), LOWEST, jnp.float32), unroll=True)
    acc_ref[...] = jnp.zeros_like(acc_ref)

    def sums(block, carry):
        high, low = split(x_factor(xy_ref, block))
        xf_ref[block, :HALF, :] = high
        xf_ref[block, HALF:, :] = low
        top = top_ref[block]
        scores = pot_of(block) - center_cost(xy_ref, block, core, rows)
        weight = jnp.exp(scores - top[:, 0:1])
        lhs = weight[:, None, :] * y_factor(xy_ref, block)[None]
        a_high, a_low = split(lhs.reshape(rows * TSIDE, lhs.shape[-1]))
        both = dot_nt(a_high, xf_ref[block])
        third = dot_nt(a_low, xf_ref[block, :HALF, :])
        part = both[:, :HALF] + both[:, HALF:] + third
        scale = jnp.where(mask_ref[block] > 0.0, jnp.exp(jnp.minimum(top - best, 0.0)), 0.0)
        acc_ref[...] += part.reshape(rows, TSIDE, HALF) * scale[:, None, :]
        return carry

    lax.fori_loop(0, blocks, sums, 0, unroll=True)
    demand = recv_ref[:, :TSIDE, :]
    return demand - best[:, None, :] - jnp.log(acc_ref[...])


def column_part(xy_ref, mask_ref, xf_ref, level, base, block, core, rows):
    active = mask_ref[block] > 0.0
    top = jnp.max(jnp.where(active, level, LOWEST), axis=1, keepdims=True)
    scale = jnp.where(active, jnp.exp(jnp.minimum(level - top, 0.0)), 0.0)
    weights = (base * scale[:, None, :]).reshape(rows * TSIDE, HALF)
    w_high, w_low = split(weights)
    mixed = dot_nn(jnp.concatenate([w_high, w_high], axis=1), xf_ref[block])
    mixed = mixed + dot_nn(w_low, xf_ref[block, :HALF, :])
    width = mixed.shape[-1]
    sums = jnp.sum(mixed.reshape(rows, TSIDE, width) * y_factor(xy_ref, block)[None], axis=1)
    tops = top - center_cost(xy_ref, block, core, rows)
    best = jnp.max(tops, axis=0, keepdims=True)
    total = jnp.sum(sums * jnp.exp(tops - best), axis=0, keepdims=True)
    return best + jnp.log(total)


def log_add(a, b):
    top = jnp.maximum(a, b)
    return top + jnp.log(jnp.exp(a - top) + jnp.exp(b - top))


def swap_minor(values):
    lane_group = lax.broadcasted_iota(jnp.int32, (TSIDE, HALF), 1) // TSIDE
    diagonal = lane_group[:COLS_HALF] == lax.broadcasted_iota(jnp.int32, (COLS_HALF, HALF), 0)
    result = []
    for b in range(TSIDE):
        start = b // COLS_HALF * HALF
        piece = jnp.where(lane_group == b % COLS_HALF, values[:, start : start + HALF], 0.0)
        for shift in (TSIDE, 2 * TSIDE, 4 * TSIDE):
            piece = piece + pltpu.roll(piece, shift, 1)
        halves = [
            jnp.sum(jnp.where(diagonal, piece[start : start + COLS_HALF], 0.0), axis=0, keepdims=True)
            for start in (0, COLS_HALF)
        ]
        result.append(halves)
    return result


def pack_kernel(devices, *refs):
    sources, message_ref, targets, sems = refs[:5], refs[5], refs[6:11], refs[11]
    copies = [
        pltpu.make_async_copy(source, target, sems.at[i])
        for i, (source, target) in enumerate(zip(sources, targets, strict=True))
    ]
    for copy in copies:
        copy.start()
    for copy in copies:
        copy.wait()
    demand_ref, cap_ref, pot_ref, pair_ref, count_ref = targets
    tiles = 2 * COLS_HALF
    tile_of = lax.broadcasted_iota(jnp.int32, (tiles, tiles), 0)
    lane_of = lax.broadcasted_iota(jnp.int32, (tiles, tiles), 1)
    counts = jnp.sum(jnp.where(tile_of == lane_of, count_ref[...], 0), axis=1, keepdims=True)
    pairs = jnp.where(lax.broadcasted_iota(jnp.int32, (tiles, KSLOTS), 1) < counts, pair_ref[...], -1)
    lanes = lax.broadcasted_iota(jnp.int32, (tiles, HALF), 1)
    found = lanes < 0
    for slot in range(KSLOTS):
        found = found | (pairs[:, slot : slot + 1] == lanes // COLS_HALF)
    own = lax.broadcasted_iota(jnp.int32, (tiles, HALF), 0) % COLS_HALF == lanes % COLS_HALF
    marks = jnp.where(found & own, 1.0, 0.0)
    grid_rows = swap_minor(demand_ref[...])
    tails = jnp.zeros((ROWS - ROW_MASK - 1, HALF), jnp.float32)
    for half in (0, 1):
        mark = jnp.sum(marks[half * COLS_HALF : (half + 1) * COLS_HALF], axis=0, keepdims=True)
        pieces = [row[half] for row in grid_rows]
        pieces += [pot_ref[:, :HALF], pot_ref[:, HALF:], cap_ref[:, :HALF], cap_ref[:, HALF:], mark, tails]
        block = jnp.concatenate(pieces, axis=0)
        for device in range(half, devices, 2):
            message_ref[device] = block


def unpack_kernel(keep_ref, got_ref, cell_ref, fac_ref):
    is_left = lax.axis_index("tile") % 2 == 0
    keep = keep_ref[:TSIDE, :]
    got = got_ref[:TSIDE, :]
    grid = jnp.concatenate([jnp.where(is_left, keep, got), jnp.where(is_left, got, keep)], axis=1)
    for row, halves in enumerate(swap_minor(grid)):
        cell_ref[row : row + 1, :HALF] = halves[0]
        cell_ref[row : row + 1, HALF:] = halves[1]
    total = log_add(keep_ref[ROW_POT : ROW_POT + 2, :], got_ref[ROW_POT : ROW_POT + 2, :])
    fac = keep_ref[ROW_CAP : ROW_CAP + 2, :] - total
    fac_ref[:, :HALF] = fac[0:1]
    fac_ref[:, HALF:] = fac[1:2]


def first_kernel(rows, blocks, recv_ref, xy_ref, part_ref, mask_ref, top_ref, xf_ref, acc_ref):
    core = lax.axis_index("tile") % 2
    build_mask(recv_ref, mask_ref, rows, blocks)

    def pot_of(block):
        return jnp.concatenate(
            [recv_ref[block, ROW_POT : ROW_POT + 1, :], recv_ref[block, ROW_POT + 1 : ROW_POT + 2, :]], axis=1
        )

    shifted = row_pass(recv_ref, xy_ref, pot_of, mask_ref, top_ref, xf_ref, acc_ref, core, rows, blocks)
    level = jnp.max(shifted, axis=1)
    acc_ref[...] = jnp.exp(shifted - level[:, None, :])

    def columns(block, carry):
        part_ref[pl.ds(block, 1), :] = column_part(
            xy_ref, mask_ref, xf_ref, level, acc_ref[...], block, core, rows
        )
        return carry

    lax.fori_loop(0, blocks, columns, 0, unroll=True)


def second_kernel(
    rows, blocks, recv_ref, xy_ref, mine_ref, other_ref, keep_ref, send_ref, pot_ref, mask_ref, top_ref, xf_ref, acc_ref
):
    me = lax.axis_index("tile")
    core = me % 2
    build_mask(recv_ref, mask_ref, rows, blocks)
    capacity = jnp.concatenate([recv_ref[:, ROW_CAP, :], recv_ref[:, ROW_CAP + 1, :]], axis=1)
    pot_ref[...] = capacity - log_add(mine_ref[...], other_ref[...])

    def pot_of(block):
        return pot_ref[pl.ds(block, 1), :]

    shifted = row_pass(recv_ref, xy_ref, pot_of, mask_ref, top_ref, xf_ref, acc_ref, core, rows, blocks)
    level = jnp.max(shifted, axis=1)
    acc_ref[...] = shifted
    x_mid = (core * HALF).astype(jnp.float32) + 0.5 * HALF
    dx = lax.broadcasted_iota(jnp.int32, (1, HALF), 1).astype(jnp.float32) - 0.5 * (HALF - 1)
    dy = lax.broadcasted_iota(jnp.int32, (TSIDE, 1), 0).astype(jnp.float32) - 0.5 * (TSIDE - 1)
    for row, out_ref in ((me, keep_ref), (me + 1 - 2 * core, send_ref)):
        y_mid = (row * TSIDE).astype(jnp.float32) + 0.5 * TSIDE
        lift = (dx * (dx + 2.0 * (x_mid - MIDDLE)) + dy * (dy + 2.0 * (y_mid - MIDDLE))) * SCALE
        out_ref[:TSIDE, :] = acc_ref[row] + lift
        part = column_part(
            xy_ref, mask_ref, xf_ref, level, jnp.exp(shifted - level[:, None, :]), row, core, rows
        )
        out_ref[ROW_POT : ROW_POT + 1, :] = part[:, :HALF]
        out_ref[ROW_POT + 1 : ROW_POT + 2, :] = part[:, HALF:]
        out_ref[ROW_CAP:, :] = recv_ref[row, ROW_CAP:, :]


def on_device_all_rows(log_demand, log_capacity, warm_potential, facility_xy, pair_block, pair_count):
    devices = lax.axis_size("tile")
    rows = devices
    blocks = facility_xy.shape[0]
    width = log_capacity.shape[1]
    light = pltpu.CompilerParams(vmem_limit_bytes=4 * 1024 * 1024)
    local = (log_demand, log_capacity, warm_potential, pair_block, pair_count.reshape(1, -1))
    local = [pltpu.with_memory_space_constraint(x, pltpu.HBM) for x in local]
    message = pl.pallas_call(
        lambda *refs: pack_kernel(devices, *refs),
        in_specs=[pl.BlockSpec(memory_space=pltpu.HBM)] * len(local),
        out_shape=jax.ShapeDtypeStruct((devices, ROWS, HALF), jnp.float32),
        scratch_shapes=[pltpu.VMEM(x.shape, x.dtype) for x in local]
        + [pltpu.SemaphoreType.DMA((len(local),))],
        compiler_params=light,
        name="pack",
    )(*local)
    recv = lax.all_to_all(message, "tile", 0, 0, tiled=True)
    scratch = [
        pltpu.VMEM((blocks, rows, HALF), jnp.float32),
        pltpu.VMEM((blocks, rows, HALF), jnp.float32),
        pltpu.VMEM((blocks, 2 * HALF, width), jnp.bfloat16),
        pltpu.VMEM((rows, TSIDE, HALF), jnp.float32),
    ]
    params = pltpu.CompilerParams(vmem_limit_bytes=32 * 1024 * 1024)
    part = pl.pallas_call(
        lambda *refs: first_kernel(rows, blocks, *refs),
        out_shape=jax.ShapeDtypeStruct((blocks, width), jnp.float32),
        scratch_shapes=scratch,
        compiler_params=params,
        name="first_iteration",
    )(recv, facility_xy)
    swap = [(i, i ^ 1) for i in range(devices)]
    other = lax.ppermute(part, "tile", swap)
    keep, send = pl.pallas_call(
        lambda *refs: second_kernel(rows, blocks, *refs),
        out_shape=(
            jax.ShapeDtypeStruct((ROWS, HALF), jnp.float32),
            jax.ShapeDtypeStruct((ROWS, HALF), jnp.float32),
        ),
        scratch_shapes=[pltpu.VMEM((blocks, width), jnp.float32)] + scratch,
        compiler_params=params,
        name="second_iteration",
    )(recv, facility_xy, part, other)
    got = lax.ppermute(send, "tile", swap)
    cell_pot, facility_pot = pl.pallas_call(
        unpack_kernel,
        out_shape=(
            jax.ShapeDtypeStruct(log_demand.shape, jnp.float32),
            jax.ShapeDtypeStruct(log_capacity.shape, jnp.float32),
        ),
        compiler_params=light,
        name="unpack",
    )(keep, got)
    return (cell_pot, facility_pot)


def from_behind(block, axis, distance):
    devices = range(lax.axis_size(axis))
    route = [(i - distance, i) for i in devices if i - distance in devices]
    return lax.ppermute(block, axis, route)


def cell_coords(tile_index):
    cell_ids = jnp.arange(TSIDE * TSIDE, dtype=jnp.int32)
    column = tile_index % TILE_COLS * TSIDE + cell_ids % TSIDE
    row_cell = tile_index // TILE_COLS * TSIDE + cell_ids // TSIDE
    return (column.astype(jnp.float32) + 0.5, row_cell.astype(jnp.float32) + 0.5)


def pair_cost(coord_x, coord_y, positions):
    delta_x = coord_x[None, :, None] - positions[:, 0, :][:, None, :]
    delta_y = coord_y[None, :, None] - positions[:, 1, :][:, None, :]
    return (delta_x * delta_x + delta_y * delta_y) / float(REACH * REACH)


def tile_pass(tile_index, demand_row, potentials, positions, active):
    coord_x, coord_y = cell_coords(tile_index)
    pair_costs = pair_cost(coord_x, coord_y, positions)
    scores = jnp.where(active[:, None, None], potentials[:, None, :] - pair_costs, LOWEST)
    row_top = jnp.max(scores, axis=(0, 2))
    row_sum = jnp.sum(jnp.exp(scores - row_top[None, :, None]), axis=(0, 2))
    cell_pot = demand_row - (row_top + jnp.log(row_sum))
    column_scores = cell_pot[None, :, None] - pair_costs
    col_top = jnp.max(column_scores, axis=1)
    col_sum = jnp.sum(jnp.exp(column_scores - col_top[:, None, :]), axis=1)
    col_top = jnp.where(active[:, None], col_top, LOWEST)
    col_sum = jnp.where(active[:, None], col_sum, 0.0)
    return (cell_pot, col_top, col_sum)


def merge_parts(top_a, sum_a, top_b, sum_b):
    top_new = jnp.maximum(top_a, top_b)
    return (top_new, sum_a * jnp.exp(top_a - top_new) + sum_b * jnp.exp(top_b - top_new))


def on_device(log_demand, log_capacity, warm_potential, facility_xy, pair_block, pair_count):
    tiles_here = log_demand.shape[0]
    blocks_here = log_capacity.shape[0]
    block_width = log_capacity.shape[1]
    devices_along = lax.axis_size("tile")
    my_index = lax.axis_index("tile")
    reach = min(devices_along - 1, (SPAN + blocks_here - 1) // blocks_here)
    window = 2 * reach + 1
    tile_ids = my_index * tiles_here + jnp.arange(tiles_here, dtype=jnp.int32)
    slot_ids = jnp.arange(KSLOTS, dtype=jnp.int32)
    first_block = (my_index - reach) * blocks_here
    local_block = pair_block - first_block
    facility_pot = warm_potential
    cell_pot = log_demand
    for step_index in range(ITERS):
        slabs = []
        for position in range(window):
            distance = reach - position
            if distance == 0:
                slabs.append(facility_pot)
            else:
                slabs.append(from_behind(facility_pot, "tile", distance))
        window_pot = jnp.concatenate(slabs, axis=0)

        def one_tile(inputs):
            tile_index, demand_row, blocks, nearby, slot_limit = inputs
            active = slot_ids < slot_limit
            return tile_pass(
                tile_index, demand_row, window_pot[nearby], facility_xy[blocks], active
            )

        cell_pot, col_top, col_sum = lax.map(
            one_tile, (tile_ids, log_demand, pair_block, local_block, pair_count)
        )
        flat_ids = local_block.reshape(-1)
        flat_top = col_top.reshape(-1, block_width)
        flat_sum = col_sum.reshape(-1, block_width)
        local_top = (
            jnp.full((window * blocks_here, block_width), LOWEST, jnp.float32)
            .at[flat_ids]
            .max(flat_top)
        )
        local_sum = (
            jnp.zeros((window * blocks_here, block_width), jnp.float32)
            .at[flat_ids]
            .add(flat_sum * jnp.exp(flat_top - local_top[flat_ids]))
        )

        def slab_of(position):
            return (
                local_top[position * blocks_here : (position + 1) * blocks_here],
                local_sum[position * blocks_here : (position + 1) * blocks_here],
            )

        own_top, block_sum = slab_of(reach)
        for distance in range(-reach, reach + 1):
            if distance != 0:
                send_top, send_sum = slab_of(reach + distance)
                got_top, got_sum = from_behind((send_top, send_sum), "tile", distance)
                source = my_index - distance
                valid = (source >= 0) & (source < devices_along)
                got_top = jnp.where(valid, got_top, LOWEST)
                got_sum = jnp.where(valid, got_sum, 0.0)
                own_top, block_sum = merge_parts(own_top, block_sum, got_top, got_sum)
        facility_pot = log_capacity - (own_top + jnp.log(block_sum))
    return (cell_pot, facility_pot)


def solution(mesh):
    placed = (
        P(("groups", "tile"), None),
        P(("groups", "tile"), None),
        P(("groups", "tile"), None),
        P("groups", None, None),
        P(("groups", "tile"), None),
        P(("groups", "tile")),
    )
    devices = mesh.shape["tile"]
    small = devices % 2 == 0 and devices * COLS_HALF == HALF

    def program(log_demand, log_capacity, warm_potential, facility_xy, pair_block, pair_count):
        one_row = log_demand.shape[0] == mesh.size * TILE_COLS and log_capacity.shape[0] == mesh.size
        fits = small and one_row and log_capacity.shape[1] == 2 * HALF
        body = on_device_all_rows if fits else on_device
        return jax.shard_map(
            body,
            mesh=mesh,
            in_specs=placed,
            out_specs=(P(("groups", "tile"), None), P(("groups", "tile"), None)),
            check_vma=False,
        )(log_demand, log_capacity, warm_potential, facility_xy, pair_block, pair_count)

    return program
```

```python
import jax
import jax.numpy as jnp
from jax import lax
from jax.experimental import pallas as pl
from jax.experimental.pallas import tpu as pltpu
from jax.sharding import PartitionSpec as P

TSIDE = 16
TILE_COLS = 16
KSLOTS = 16
ITERS = 2
REACH = 64
SPAN = 16


LOWEST = -1e30

HALF = TSIDE * TILE_COLS // 2
COLS_HALF = TILE_COLS // 2
SCALE = 1.0 / float(REACH * REACH)
MIDDLE = 736.0
TAIL = 8
ROWS = 2 * TSIDE + TAIL
KEEP_ROWS = TSIDE + TAIL
ROW_POT = 0
ROW_CAP = 2
ROW_MASK = 4
STEP = 4


def dot_nt(a, b):
    return lax.dot_general(a, b, (((1,), (1,)), ((), ())), preferred_element_type=jnp.float32)


def dot_nn(a, b):
    return lax.dot_general(a, b, (((1,), (0,)), ((), ())), preferred_element_type=jnp.float32)


def split(values):
    high = values.astype(jnp.bfloat16)
    low = (values - high.astype(jnp.float32)).astype(jnp.bfloat16)
    return high, low


def halves_of(row_pair):
    return jnp.concatenate([row_pair[0:1, :], row_pair[1:2, :]], axis=1)


class Gathered:
    def __init__(self, refs):
        self.refs = refs
        self.slots = range(len(refs) * refs[0].shape[0])

    def block_of(self, slot, first, rows):
        return self.refs[slot % STEP][slot // STEP, first : first + rows, :]

    def demand(self, slot):
        return self.block_of(slot, TAIL if slot % 2 else 0, TSIDE)

    def tail(self, slot):
        return self.block_of(slot, 0 if slot % 2 else TSIDE, TAIL)

    def potential(self, slot):
        return halves_of(self.tail(slot)[ROW_POT : ROW_POT + 2])

    def capacity(self, slot):
        return halves_of(self.tail(slot)[ROW_CAP : ROW_CAP + 2])

    def mask(self, slot):
        row = ROW_MASK + slot % 2
        return self.tail(slot)[row : row + 1]


def setup_kernel(slots, xy_ref, xf_ref, yf_ref, cost_ref):
    me = lax.axis_index("tile")
    x_mid = (me % 2 * HALF).astype(jnp.float32) + 0.5 * HALF
    row_ids = me ^ lax.broadcasted_iota(jnp.int32, (slots, 1), 0)
    y_mid = (row_ids * TSIDE).astype(jnp.float32) + 0.5 * TSIDE
    x_off = lax.broadcasted_iota(jnp.int32, (HALF, 1), 0).astype(jnp.float32) - 0.5 * (HALF - 1)
    y_off = lax.broadcasted_iota(jnp.int32, (TSIDE, 1), 0).astype(jnp.float32) - 0.5 * (TSIDE - 1)
    for slot in range(slots):
        block = me ^ slot
        fx = xy_ref[block, 0:1, :]
        fy = xy_ref[block, 1:2, :]
        high, low = split(jnp.exp(x_off * ((fx - MIDDLE) * (2.0 * SCALE))))
        xf_ref[slot, :HALF, :] = high
        xf_ref[slot, HALF:, :] = low
        yf_ref[slot] = jnp.exp(y_off * ((fy - MIDDLE) * (2.0 * SCALE)))
        dx = x_mid - fx
        dy = y_mid - fy
        cost_ref[slot] = (dx * dx + dy * dy) * SCALE


def build_mask(gathered, me, mask_ref):
    slots = len(gathered.slots)
    marks = jnp.concatenate([gathered.mask(slot) for slot in gathered.slots], axis=0)
    lane_block = lax.broadcasted_iota(jnp.int32, (slots, slots, HALF), 2) // COLS_HALF
    own_block = lax.broadcasted_iota(jnp.int32, (slots, slots, HALF), 0) ^ me
    picked = jnp.where(lane_block == own_block, marks[None], 0.0)
    picked = picked.reshape(slots * slots, HALF).astype(jnp.bfloat16)
    source = lax.broadcasted_iota(jnp.int32, (HALF, HALF), 0) % COLS_HALF
    target = lax.broadcasted_iota(jnp.int32, (HALF, HALF), 1) // TSIDE
    spread = jnp.where(source == target, 1.0, 0.0).astype(jnp.bfloat16)
    mask_ref[...] = dot_nn(picked, spread).reshape(slots, slots, HALF)


def row_pass(gathered, potential, factors, mask_ref, acc_ref):
    xf_ref, yf_ref, cost_ref = factors
    slots = len(gathered.slots)
    best = jnp.full((slots, HALF), LOWEST, jnp.float32)
    tops = []
    for slot in gathered.slots:
        top = jnp.max(potential(slot) - cost_ref[slot], axis=1, keepdims=True)
        tops.append(top)
        best = jnp.maximum(best, jnp.where(mask_ref[slot] > 0.0, top, LOWEST))
    for slot in gathered.slots:
        top = tops[slot]
        weight = jnp.exp(potential(slot) - cost_ref[slot] - top)
        lhs = weight[:, None, :] * yf_ref[slot][None]
        a_high, a_low = split(lhs.reshape(slots * TSIDE, lhs.shape[-1]))
        both = dot_nt(a_high, xf_ref[slot])
        third = dot_nt(a_low, xf_ref[slot, :HALF, :])
        part = both[:, :HALF] + both[:, HALF:] + third
        scale = jnp.where(mask_ref[slot] > 0.0, jnp.exp(jnp.minimum(top - best, 0.0)), 0.0)
        scaled = part.reshape(slots, TSIDE, HALF) * scale[:, None, :]
        if slot == 0:
            acc_ref[...] = scaled
        else:
            acc_ref[...] += scaled
    demand = jnp.concatenate([gathered.demand(slot)[None] for slot in gathered.slots], axis=0)
    return demand - best[:, None, :] - jnp.log(acc_ref[...])


def column_part(factors, mask_ref, level, base, slot):
    xf_ref, yf_ref, cost_ref = factors
    slots = level.shape[0]
    active = mask_ref[slot] > 0.0
    top = jnp.max(jnp.where(active, level, LOWEST), axis=1, keepdims=True)
    scale = jnp.where(active, jnp.exp(jnp.minimum(level - top, 0.0)), 0.0)
    weights = (base * scale[:, None, :]).reshape(slots * TSIDE, HALF)
    w_high, w_low = split(weights)
    mixed = dot_nn(jnp.concatenate([w_high, w_high], axis=1), xf_ref[slot])
    mixed = mixed + dot_nn(w_low, xf_ref[slot, :HALF, :])
    width = mixed.shape[-1]
    sums = jnp.sum(mixed.reshape(slots, TSIDE, width) * yf_ref[slot][None], axis=1)
    tops = top - cost_ref[slot]
    best = jnp.max(tops, axis=0, keepdims=True)
    total = jnp.sum(sums * jnp.exp(tops - best), axis=0, keepdims=True)
    return best + jnp.log(total)


def log_add(a, b):
    top = jnp.maximum(a, b)
    return top + jnp.log(jnp.exp(a - top) + jnp.exp(b - top))


def swap_minor(values):
    lane_group = lax.broadcasted_iota(jnp.int32, (TSIDE, HALF), 1) // TSIDE
    diagonal = lane_group[:COLS_HALF] == lax.broadcasted_iota(jnp.int32, (COLS_HALF, HALF), 0)
    result = []
    for b in range(TSIDE):
        start = b // COLS_HALF * HALF
        piece = jnp.where(lane_group == b % COLS_HALF, values[:, start : start + HALF], 0.0)
        for shift in (TSIDE, 2 * TSIDE, 4 * TSIDE):
            piece = piece + pltpu.roll(piece, shift, 1)
        halves = [
            jnp.sum(jnp.where(diagonal, piece[start : start + COLS_HALF], 0.0), axis=0, keepdims=True)
            for start in (0, COLS_HALF)
        ]
        result.append(halves)
    return result


def pack_kernel(*refs):
    sources, message_ref, targets, sems = refs[:5], refs[5], refs[6:11], refs[11]
    copies = [
        pltpu.make_async_copy(source, target, sems.at[i])
        for i, (source, target) in enumerate(zip(sources, targets, strict=True))
    ]
    for copy in copies:
        copy.start()
    for copy in copies:
        copy.wait()
    demand_ref, cap_ref, pot_ref, pair_ref, count_ref = targets
    tiles = 2 * COLS_HALF
    tile_of = lax.broadcasted_iota(jnp.int32, (tiles, tiles), 0)
    lane_of = lax.broadcasted_iota(jnp.int32, (tiles, tiles), 1)
    counts = jnp.sum(jnp.where(tile_of == lane_of, count_ref[...], 0), axis=1, keepdims=True)
    pairs = jnp.where(lax.broadcasted_iota(jnp.int32, (tiles, KSLOTS), 1) < counts, pair_ref[...], -1)
    lanes = lax.broadcasted_iota(jnp.int32, (tiles, HALF), 1)
    found = lanes < 0
    for slot in range(KSLOTS):
        found = found | (pairs[:, slot : slot + 1] == lanes // COLS_HALF)
    own = lax.broadcasted_iota(jnp.int32, (tiles, HALF), 0) % COLS_HALF == lanes % COLS_HALF
    marks = jnp.where(found & own, 1.0, 0.0)
    grid_rows = swap_minor(demand_ref[...])
    is_left = lax.axis_index("tile") % 2 == 0
    tops = [jnp.sum(marks[start : start + COLS_HALF], axis=0, keepdims=True) for start in (0, COLS_HALF)]
    sides = [jnp.concatenate([row[half] for row in grid_rows], axis=0) for half in (0, 1)]
    message_ref[:TSIDE, :] = jnp.where(is_left, sides[0], sides[1])
    message_ref[TSIDE + TAIL :, :] = jnp.where(is_left, sides[1], sides[0])
    pieces = [pot_ref[:, :HALF], pot_ref[:, HALF:], cap_ref[:, :HALF], cap_ref[:, HALF:]]
    pieces += [jnp.where(is_left, tops[0], tops[1]), jnp.where(is_left, tops[1], tops[0])]
    pieces += [jnp.zeros((TAIL - ROW_MASK - 2, HALF), jnp.float32)]
    message_ref[TSIDE : TSIDE + TAIL, :] = jnp.concatenate(pieces, axis=0)


def unpack_kernel(keep_ref, got_ref, cell_ref, fac_ref):
    is_left = lax.axis_index("tile") % 2 == 0
    keep = keep_ref[:TSIDE, :]
    got = got_ref[:TSIDE, :]
    grid = jnp.concatenate([jnp.where(is_left, keep, got), jnp.where(is_left, got, keep)], axis=1)
    for row, halves in enumerate(swap_minor(grid)):
        cell_ref[row : row + 1, :HALF] = halves[0]
        cell_ref[row : row + 1, HALF:] = halves[1]
    tail = keep_ref[TSIDE:, :]
    total = log_add(tail[ROW_POT : ROW_POT + 2], got_ref[TSIDE + ROW_POT : TSIDE + ROW_POT + 2, :])
    fac = tail[ROW_CAP : ROW_CAP + 2] - total
    fac_ref[:, :HALF] = fac[0:1]
    fac_ref[:, HALF:] = fac[1:2]


def first_kernel(*refs):
    gathered = Gathered(refs[:STEP])
    factors = refs[STEP : STEP + 3]
    part_ref, mask_ref, acc_ref = refs[STEP + 3 :]
    build_mask(gathered, lax.axis_index("tile"), mask_ref)
    shifted = row_pass(gathered, gathered.potential, factors, mask_ref, acc_ref)
    level = jnp.max(shifted, axis=1)
    acc_ref[...] = jnp.exp(shifted - level[:, None, :])
    for slot in gathered.slots:
        part_ref[slot : slot + 1, :] = column_part(factors, mask_ref, level, acc_ref[...], slot)


def second_kernel(*refs):
    gathered = Gathered(refs[:STEP])
    factors = refs[STEP : STEP + 3]
    mine_ref, other_ref, keep_ref, send_ref, pot_ref, mask_ref, acc_ref = refs[STEP + 3 :]
    me = lax.axis_index("tile")
    core = me % 2
    build_mask(gathered, me, mask_ref)
    slots = len(gathered.slots)
    other = other_ref[...]
    even = lax.broadcasted_iota(jnp.int32, other.shape, 0) % 2 == 0
    swapped = jnp.where(even, pltpu.roll(other, slots - 1, 0), pltpu.roll(other, 1, 0))
    capacity = jnp.concatenate([gathered.capacity(slot) for slot in gathered.slots], axis=0)
    pot_ref[...] = capacity - log_add(mine_ref[...], swapped)

    def potential(slot):
        return pot_ref[slot : slot + 1, :]

    shifted = row_pass(gathered, potential, factors, mask_ref, acc_ref)
    level = jnp.max(shifted, axis=1)
    base = jnp.exp(shifted - level[:, None, :])
    x_mid = (core * HALF).astype(jnp.float32) + 0.5 * HALF
    dx = lax.broadcasted_iota(jnp.int32, (1, HALF), 1).astype(jnp.float32) - 0.5 * (HALF - 1)
    dy = lax.broadcasted_iota(jnp.int32, (TSIDE, 1), 0).astype(jnp.float32) - 0.5 * (TSIDE - 1)
    for slot, out_ref in ((0, keep_ref), (1, send_ref)):
        y_mid = ((me ^ slot) * TSIDE).astype(jnp.float32) + 0.5 * TSIDE
        lift = (dx * (dx + 2.0 * (x_mid - MIDDLE)) + dy * (dy + 2.0 * (y_mid - MIDDLE))) * SCALE
        out_ref[:TSIDE, :] = shifted[slot] + lift
        part = column_part(factors, mask_ref, level, base, slot)
        pieces = [part[:, :HALF], part[:, HALF:], gathered.tail(slot)[ROW_CAP:]]
        out_ref[TSIDE:, :] = jnp.concatenate(pieces, axis=0)


def exchange(block, distance):
    devices = lax.axis_size("tile")
    return lax.ppermute(block, "tile", [(i, i ^ distance) for i in range(devices)])


def on_device_all_rows(log_demand, log_capacity, warm_potential, facility_xy, pair_block, pair_count):
    slots = lax.axis_size("tile")
    width = log_capacity.shape[1]
    light = pltpu.CompilerParams(vmem_limit_bytes=4 * 1024 * 1024)
    heavy = pltpu.CompilerParams(vmem_limit_bytes=16 * 1024 * 1024)
    local = (log_demand, log_capacity, warm_potential, pair_block, pair_count.reshape(1, -1))
    local = [pltpu.with_memory_space_constraint(x, pltpu.HBM) for x in local]
    message = pl.pallas_call(
        pack_kernel,
        in_specs=[pl.BlockSpec(memory_space=pltpu.HBM)] * len(local),
        out_shape=jax.ShapeDtypeStruct((ROWS, HALF), jnp.float32),
        scratch_shapes=[pltpu.VMEM(x.shape, x.dtype) for x in local]
        + [pltpu.SemaphoreType.DMA((len(local),))],
        compiler_params=light,
        name="pack",
    )(*local)
    factors = pl.pallas_call(
        lambda *refs: setup_kernel(slots, *refs),
        out_shape=(
            jax.ShapeDtypeStruct((slots, 2 * HALF, width), jnp.bfloat16),
            jax.ShapeDtypeStruct((slots, TSIDE, width), jnp.float32),
            jax.ShapeDtypeStruct((slots, slots, width), jnp.float32),
        ),
        compiler_params=light,
        name="setup",
    )(facility_xy)
    lines = message[None]
    distance = STEP
    while distance < slots:
        lines = jnp.concatenate([lines, exchange(lines, distance)], axis=0)
        distance *= 2
    same = lines[:, :KEEP_ROWS]
    across = lines[:, TSIDE:]
    gathered = (lines, exchange(across, 1), exchange(same, 2), exchange(across, 3))
    scratch = [
        pltpu.VMEM((slots, slots, HALF), jnp.float32),
        pltpu.VMEM((slots, TSIDE, HALF), jnp.float32),
    ]
    part = pl.pallas_call(
        first_kernel,
        out_shape=jax.ShapeDtypeStruct((slots, width), jnp.float32),
        scratch_shapes=scratch,
        compiler_params=heavy,
        name="first_iteration",
    )(*gathered, *factors)
    other = exchange(part, 1)
    keep, send = pl.pallas_call(
        second_kernel,
        out_shape=(
            jax.ShapeDtypeStruct((KEEP_ROWS, HALF), jnp.float32),
            jax.ShapeDtypeStruct((KEEP_ROWS, HALF), jnp.float32),
        ),
        scratch_shapes=[pltpu.VMEM((slots, width), jnp.float32)] + scratch,
        compiler_params=heavy,
        name="second_iteration",
    )(*gathered, *factors, part, other)
    got = exchange(send, 1)
    return pl.pallas_call(
        unpack_kernel,
        out_shape=(
            jax.ShapeDtypeStruct(log_demand.shape, jnp.float32),
            jax.ShapeDtypeStruct(log_capacity.shape, jnp.float32),
        ),
        compiler_params=light,
        name="unpack",
    )(keep, got)


def from_behind(block, axis, distance):
    devices = range(lax.axis_size(axis))
    route = [(i - distance, i) for i in devices if i - distance in devices]
    return lax.ppermute(block, axis, route)


def cell_coords(tile_index):
    cell_ids = jnp.arange(TSIDE * TSIDE, dtype=jnp.int32)
    column = tile_index % TILE_COLS * TSIDE + cell_ids % TSIDE
    row_cell = tile_index // TILE_COLS * TSIDE + cell_ids // TSIDE
    return (column.astype(jnp.float32) + 0.5, row_cell.astype(jnp.float32) + 0.5)


def pair_cost(coord_x, coord_y, positions):
    delta_x = coord_x[None, :, None] - positions[:, 0, :][:, None, :]
    delta_y = coord_y[None, :, None] - positions[:, 1, :][:, None, :]
    return (delta_x * delta_x + delta_y * delta_y) / float(REACH * REACH)


def tile_pass(tile_index, demand_row, potentials, positions, active):
    coord_x, coord_y = cell_coords(tile_index)
    pair_costs = pair_cost(coord_x, coord_y, positions)
    scores = jnp.where(active[:, None, None], potentials[:, None, :] - pair_costs, LOWEST)
    row_top = jnp.max(scores, axis=(0, 2))
    row_sum = jnp.sum(jnp.exp(scores - row_top[None, :, None]), axis=(0, 2))
    cell_pot = demand_row - (row_top + jnp.log(row_sum))
    column_scores = cell_pot[None, :, None] - pair_costs
    col_top = jnp.max(column_scores, axis=1)
    col_sum = jnp.sum(jnp.exp(column_scores - col_top[:, None, :]), axis=1)
    col_top = jnp.where(active[:, None], col_top, LOWEST)
    col_sum = jnp.where(active[:, None], col_sum, 0.0)
    return (cell_pot, col_top, col_sum)


def merge_parts(top_a, sum_a, top_b, sum_b):
    top_new = jnp.maximum(top_a, top_b)
    return (top_new, sum_a * jnp.exp(top_a - top_new) + sum_b * jnp.exp(top_b - top_new))


def on_device(log_demand, log_capacity, warm_potential, facility_xy, pair_block, pair_count):
    tiles_here = log_demand.shape[0]
    blocks_here = log_capacity.shape[0]
    block_width = log_capacity.shape[1]
    devices_along = lax.axis_size("tile")
    my_index = lax.axis_index("tile")
    reach = min(devices_along - 1, (SPAN + blocks_here - 1) // blocks_here)
    window = 2 * reach + 1
    tile_ids = my_index * tiles_here + jnp.arange(tiles_here, dtype=jnp.int32)
    slot_ids = jnp.arange(KSLOTS, dtype=jnp.int32)
    first_block = (my_index - reach) * blocks_here
    local_block = pair_block - first_block
    facility_pot = warm_potential
    cell_pot = log_demand
    for step_index in range(ITERS):
        slabs = []
        for position in range(window):
            distance = reach - position
            if distance == 0:
                slabs.append(facility_pot)
            else:
                slabs.append(from_behind(facility_pot, "tile", distance))
        window_pot = jnp.concatenate(slabs, axis=0)

        def one_tile(inputs):
            tile_index, demand_row, blocks, nearby, slot_limit = inputs
            active = slot_ids < slot_limit
            return tile_pass(
                tile_index, demand_row, window_pot[nearby], facility_xy[blocks], active
            )

        cell_pot, col_top, col_sum = lax.map(
            one_tile, (tile_ids, log_demand, pair_block, local_block, pair_count)
        )
        flat_ids = local_block.reshape(-1)
        flat_top = col_top.reshape(-1, block_width)
        flat_sum = col_sum.reshape(-1, block_width)
        local_top = (
            jnp.full((window * blocks_here, block_width), LOWEST, jnp.float32)
            .at[flat_ids]
            .max(flat_top)
        )
        local_sum = (
            jnp.zeros((window * blocks_here, block_width), jnp.float32)
            .at[flat_ids]
            .add(flat_sum * jnp.exp(flat_top - local_top[flat_ids]))
        )

        def slab_of(position):
            return (
                local_top[position * blocks_here : (position + 1) * blocks_here],
                local_sum[position * blocks_here : (position + 1) * blocks_here],
            )

        own_top, block_sum = slab_of(reach)
        for distance in range(-reach, reach + 1):
            if distance != 0:
                send_top, send_sum = slab_of(reach + distance)
                got_top, got_sum = from_behind((send_top, send_sum), "tile", distance)
                source = my_index - distance
                valid = (source >= 0) & (source < devices_along)
                got_top = jnp.where(valid, got_top, LOWEST)
                got_sum = jnp.where(valid, got_sum, 0.0)
                own_top, block_sum = merge_parts(own_top, block_sum, got_top, got_sum)
        facility_pot = log_capacity - (own_top + jnp.log(block_sum))
    return (cell_pot, facility_pot)


def solution(mesh):
    placed = (
        P(("groups", "tile"), None),
        P(("groups", "tile"), None),
        P(("groups", "tile"), None),
        P("groups", None, None),
        P(("groups", "tile"), None),
        P(("groups", "tile")),
    )
    devices = mesh.shape["tile"]
    small = devices % 2 == 0 and devices * COLS_HALF == HALF

    def program(log_demand, log_capacity, warm_potential, facility_xy, pair_block, pair_count):
        one_row = log_demand.shape[0] == mesh.size * TILE_COLS and log_capacity.shape[0] == mesh.size
        fits = small and one_row and log_capacity.shape[1] == 2 * HALF
        body = on_device_all_rows if fits else on_device
        return jax.shard_map(
            body,
            mesh=mesh,
            in_specs=placed,
            out_specs=(P(("groups", "tile"), None), P(("groups", "tile"), None)),
            check_vma=False,
        )(log_demand, log_capacity, warm_potential, facility_xy, pair_block, pair_count)

    return program
```

```python
import jax
import jax.numpy as jnp
from jax import lax
from jax.experimental import pallas as pl
from jax.experimental.pallas import tpu as pltpu
from jax.sharding import PartitionSpec as P

TSIDE = 16
TILE_COLS = 16
KSLOTS = 16
ITERS = 2
REACH = 64
SPAN = 16


LOWEST = -1e30

HALF = TSIDE * TILE_COLS // 2
COLS_HALF = TILE_COLS // 2
SCALE = 1.0 / float(REACH * REACH)
MIDDLE = 736.0
TAIL = 8
ROWS = 2 * TSIDE + TAIL
KEEP_ROWS = TSIDE + TAIL
ROW_POT = 0
ROW_CAP = 2
ROW_MASK = 4
STEP = 4
SUBLANES = 8
LOG2E = 1.4426950408889634
LN2 = 0.6931471805599453


def dot_nt(a, b):
    return lax.dot_general(a, b, (((1,), (1,)), ((), ())), preferred_element_type=jnp.float32)


def dot_nn(a, b):
    return lax.dot_general(a, b, (((1,), (0,)), ((), ())), preferred_element_type=jnp.float32)


def split(values):
    high = values.astype(jnp.bfloat16)
    low = (values - high.astype(jnp.float32)).astype(jnp.bfloat16)
    return high, low


def halves_of(row_pair):
    return jnp.concatenate([row_pair[0:1, :], row_pair[1:2, :]], axis=1)


class Gathered:
    def __init__(self, refs):
        self.refs = refs
        self.slots = range(len(refs) * refs[0].shape[0])

    def block_of(self, slot, first, rows):
        return self.refs[slot % STEP][slot // STEP, first : first + rows, :]

    def demand(self, slot):
        return self.block_of(slot, TAIL if slot % 2 else 0, TSIDE)

    def tail(self, slot):
        return self.block_of(slot, 0 if slot % 2 else TSIDE, TAIL)

    def potential(self, slot):
        return halves_of(self.tail(slot)[ROW_POT : ROW_POT + 2])

    def capacity(self, slot):
        return halves_of(self.tail(slot)[ROW_CAP : ROW_CAP + 2])

    def mask(self, slot):
        row = ROW_MASK + slot % 2
        return self.tail(slot)[row : row + 1]


def setup_kernel(slots, xy_ref, xf_ref, yf_ref, cost_ref):
    me = lax.axis_index("tile")
    x_mid = (me % 2 * HALF).astype(jnp.float32) + 0.5 * HALF
    row_ids = me ^ lax.broadcasted_iota(jnp.int32, (slots, 1), 0)
    y_mid = (row_ids * TSIDE).astype(jnp.float32) + 0.5 * TSIDE
    x_off = lax.broadcasted_iota(jnp.int32, (HALF, 1), 0).astype(jnp.float32) - 0.5 * (HALF - 1)
    y_off = lax.broadcasted_iota(jnp.int32, (TSIDE, 1), 0).astype(jnp.float32) - 0.5 * (TSIDE - 1)
    for slot in range(slots):
        block = me ^ slot
        fx = xy_ref[block, 0:1, :]
        fy = xy_ref[block, 1:2, :]
        high, low = split(jnp.exp(x_off * ((fx - MIDDLE) * (2.0 * SCALE))))
        xf_ref[slot, :HALF, :] = high
        xf_ref[slot, HALF:, :] = low
        y_factor = jnp.exp(y_off * ((fy - MIDDLE) * (2.0 * SCALE)))
        yf_ref[slot] = jnp.broadcast_to(y_factor[:, None, :], yf_ref.shape[1:])
        dx = x_mid - fx
        dy = y_mid - fy
        cost_ref[slot] = (dx * dx + dy * dy) * SCALE


def build_mask(gathered, me, mask_ref):
    slots = len(gathered.slots)
    marks = jnp.concatenate([gathered.mask(slot) for slot in gathered.slots], axis=0)
    lane_block = lax.broadcasted_iota(jnp.int32, (slots, slots, HALF), 2) // COLS_HALF
    own_block = lax.broadcasted_iota(jnp.int32, (slots, slots, HALF), 0) ^ me
    picked = jnp.where(lane_block == own_block, marks[None], 0.0)
    picked = picked.reshape(slots * slots, HALF).astype(jnp.bfloat16)
    source = lax.broadcasted_iota(jnp.int32, (HALF, HALF), 0) % COLS_HALF
    target = lax.broadcasted_iota(jnp.int32, (HALF, HALF), 1) // TSIDE
    spread = jnp.where(source == target, 1.0, 0.0).astype(jnp.bfloat16)
    mask_ref[...] = dot_nn(picked, spread).reshape(slots, slots, HALF)


def block_top(potential, factors, slot):
    return jnp.max(potential(slot) - factors[2][slot], axis=1, keepdims=True)


def block_sums(potential, factors, top, slot):
    xf_ref, yf_ref, cost_ref = factors
    slots = top.shape[0]
    weight = jnp.exp(potential(slot) - cost_ref[slot] - top)
    parts = [weight[i : i + SUBLANES][None] * yf_ref[slot] for i in range(0, slots, SUBLANES)]
    lhs = jnp.concatenate(parts, axis=1)
    a_high, a_low = split(lhs.reshape(TSIDE * slots, lhs.shape[-1]))
    return row_product(a_high, a_low, xf_ref, slot).reshape(TSIDE, slots, HALF)


def row_pass(potential, factors, mask_ref, demand_ref, acc_ref, early_ref=None):
    slots = mask_ref.shape[0]
    best = jnp.full((slots, HALF), LOWEST, jnp.float32)
    tops = []
    for slot in range(slots):
        top = block_top(potential, factors, slot)
        tops.append(top)
        best = jnp.maximum(best, jnp.where(mask_ref[slot] > 0.0, top, LOWEST))
    for slot in range(slots):
        top = tops[slot]
        if early_ref is not None and slot % STEP == 0:
            part = early_ref[slot // STEP]
        else:
            part = block_sums(potential, factors, top, slot)
        scale = jnp.where(mask_ref[slot] > 0.0, jnp.exp(jnp.minimum(top - best, 0.0)), 0.0)
        scaled = part * scale[None]
        if slot == 0:
            acc_ref[...] = scaled
        else:
            acc_ref[...] += scaled
    return demand_ref[...] - best[None] - jnp.log(acc_ref[...])


def row_product(a_high, a_low, xf_ref, slot):
    both = dot_nt(a_high, xf_ref[slot])
    third = dot_nt(a_low, xf_ref[slot, :HALF, :])
    return both[:, :HALF] + both[:, HALF:] + third


def column_product(w_high, w_low, xf_ref, slot):
    mixed = dot_nn(jnp.concatenate([w_high, w_high], axis=1), xf_ref[slot])
    return mixed + dot_nn(w_low, xf_ref[slot, :HALF, :])


def column_base(shifted):
    scaled = shifted * LOG2E
    level = jnp.ceil(jnp.max(scaled, axis=0))
    high, low = split(jnp.exp2(scaled - level[None]))
    return level, high, low


def column_part(factors, mask_ref, base, slot):
    xf_ref, yf_ref, cost_ref = factors
    level, high, low = base
    slots = level.shape[0]
    active = mask_ref[slot] > 0.0
    top = jnp.max(jnp.where(active, level, LOWEST), axis=1, keepdims=True)
    scale = jnp.where(active, jnp.exp2(jnp.minimum(level - top, 0.0)), 0.0).astype(jnp.bfloat16)
    w_high = (high * scale[None]).reshape(TSIDE * slots, HALF)
    w_low = (low * scale[None]).reshape(TSIDE * slots, HALF)
    mixed = column_product(w_high, w_low, xf_ref, slot)
    mixed = mixed.reshape(TSIDE, slots, mixed.shape[-1])
    sums = [
        jnp.sum(mixed[:, i : i + SUBLANES] * yf_ref[slot], axis=0) for i in range(0, slots, SUBLANES)
    ]
    sums = jnp.concatenate(sums, axis=0)
    tops = top * LN2 - cost_ref[slot]
    best = jnp.max(tops, axis=0, keepdims=True)
    total = jnp.sum(sums * jnp.exp(tops - best), axis=0, keepdims=True)
    return best + jnp.log(total)


def log_add(a, b):
    top = jnp.maximum(a, b)
    return top + jnp.log(jnp.exp(a - top) + jnp.exp(b - top))


def swap_minor(values):
    lane_group = lax.broadcasted_iota(jnp.int32, (TSIDE, HALF), 1) // TSIDE
    diagonal = lane_group[:COLS_HALF] == lax.broadcasted_iota(jnp.int32, (COLS_HALF, HALF), 0)
    result = []
    for b in range(TSIDE):
        start = b // COLS_HALF * HALF
        piece = jnp.where(lane_group == b % COLS_HALF, values[:, start : start + HALF], 0.0)
        for shift in (TSIDE, 2 * TSIDE, 4 * TSIDE):
            piece = piece + pltpu.roll(piece, shift, 1)
        halves = [
            jnp.sum(jnp.where(diagonal, piece[start : start + COLS_HALF], 0.0), axis=0, keepdims=True)
            for start in (0, COLS_HALF)
        ]
        result.append(halves)
    return result


def swap_half(values):
    lane_group = lax.broadcasted_iota(jnp.int32, (TSIDE, HALF), 1) // TSIDE
    diagonal = lane_group[:COLS_HALF] == lax.broadcasted_iota(jnp.int32, (COLS_HALF, HALF), 0)
    result = ([], [])
    for tile in range(COLS_HALF):
        piece = jnp.where(lane_group == tile, values, 0.0)
        for shift in (TSIDE, 2 * TSIDE, 4 * TSIDE):
            piece = piece + pltpu.roll(piece, shift, 1)
        for half in (0, 1):
            part = piece[half * COLS_HALF : (half + 1) * COLS_HALF]
            result[half].append(jnp.sum(jnp.where(diagonal, part, 0.0), axis=0, keepdims=True))
    return jnp.concatenate(result[0] + result[1], axis=0)


def pack_kernel(*refs):
    sources, message_ref, targets, sems = refs[:5], refs[5], refs[6:11], refs[11]
    copies = [
        pltpu.make_async_copy(source, target, sems.at[i])
        for i, (source, target) in enumerate(zip(sources, targets, strict=True))
    ]
    for copy in copies:
        copy.start()
    for copy in copies:
        copy.wait()
    demand_ref, cap_ref, pot_ref, pair_ref, count_ref = targets
    tiles = 2 * COLS_HALF
    tile_of = lax.broadcasted_iota(jnp.int32, (tiles, tiles), 0)
    lane_of = lax.broadcasted_iota(jnp.int32, (tiles, tiles), 1)
    counts = jnp.sum(jnp.where(tile_of == lane_of, count_ref[...], 0), axis=1, keepdims=True)
    pairs = jnp.where(lax.broadcasted_iota(jnp.int32, (tiles, KSLOTS), 1) < counts, pair_ref[...], -1)
    lanes = lax.broadcasted_iota(jnp.int32, (tiles, HALF), 1)
    found = lanes < 0
    for slot in range(KSLOTS):
        found = found | (pairs[:, slot : slot + 1] == lanes // COLS_HALF)
    own = lax.broadcasted_iota(jnp.int32, (tiles, HALF), 0) % COLS_HALF == lanes % COLS_HALF
    marks = jnp.where(found & own, 1.0, 0.0)
    grid_rows = swap_minor(demand_ref[...])
    is_left = lax.axis_index("tile") % 2 == 0
    tops = [jnp.sum(marks[start : start + COLS_HALF], axis=0, keepdims=True) for start in (0, COLS_HALF)]
    sides = [jnp.concatenate([row[half] for row in grid_rows], axis=0) for half in (0, 1)]
    message_ref[:TSIDE, :] = jnp.where(is_left, sides[0], sides[1])
    message_ref[TSIDE + TAIL :, :] = jnp.where(is_left, sides[1], sides[0])
    pieces = [pot_ref[:, :HALF], pot_ref[:, HALF:], cap_ref[:, :HALF], cap_ref[:, HALF:]]
    pieces += [jnp.where(is_left, tops[0], tops[1]), jnp.where(is_left, tops[1], tops[0])]
    pieces += [jnp.zeros((TAIL - ROW_MASK - 2, HALF), jnp.float32)]
    message_ref[TSIDE : TSIDE + TAIL, :] = jnp.concatenate(pieces, axis=0)


def unpack_kernel(keep_ref, got_ref, cell_ref, fac_ref):
    core = lax.axis_index("tile") % 2
    for side, ref in ((core, keep_ref), (1 - core, got_ref)):
        rows = pl.ds(pl.multiple_of(side * COLS_HALF, COLS_HALF), COLS_HALF)
        cell_ref[rows, :HALF] = ref[:COLS_HALF, :]
        cell_ref[rows, HALF:] = ref[COLS_HALF:TSIDE, :]
    tail = keep_ref[TSIDE:, :]
    total = log_add(tail[ROW_POT : ROW_POT + 2], got_ref[TSIDE + ROW_POT : TSIDE + ROW_POT + 2, :])
    fac = tail[ROW_CAP : ROW_CAP + 2] - total
    fac_ref[:, :HALF] = fac[0:1]
    fac_ref[:, HALF:] = fac[1:2]


def early_kernel(*refs):
    gathered = Gathered(refs[:1])
    factors = refs[1:4]
    for line in range(refs[0].shape[0]):
        slot = line * STEP
        top = block_top(gathered.potential, factors, slot)
        refs[4][line] = block_sums(gathered.potential, factors, top, slot)


def first_kernel(*refs):
    gathered = Gathered(refs[:STEP])
    factors = refs[STEP : STEP + 3]
    early_ref, part_ref, mask_ref, demand_ref, cap_ref, acc_ref = refs[STEP + 3 :]
    build_mask(gathered, lax.axis_index("tile"), mask_ref)
    for slot in gathered.slots:
        demand_ref[:, slot, :] = gathered.demand(slot)
        cap_ref[slot : slot + 1, :] = gathered.capacity(slot)
    base = column_base(row_pass(gathered.potential, factors, mask_ref, demand_ref, acc_ref, early_ref))
    for slot in gathered.slots:
        part_ref[slot : slot + 1, :] = column_part(factors, mask_ref, base, slot)


def second_kernel(*refs):
    factors = refs[:3]
    mask_ref, demand_ref, cap_ref, mine_ref, other_ref, keep_ref, send_ref, pot_ref, acc_ref = refs[3:]
    me = lax.axis_index("tile")
    core = me % 2
    slots = mask_ref.shape[0]
    other = other_ref[...]
    even = lax.broadcasted_iota(jnp.int32, other.shape, 0) % 2 == 0
    swapped = jnp.where(even, pltpu.roll(other, slots - 1, 0), pltpu.roll(other, 1, 0))
    pot_ref[...] = cap_ref[...] - log_add(mine_ref[...], swapped)

    def potential(slot):
        return pot_ref[slot : slot + 1, :]

    shifted = row_pass(potential, factors, mask_ref, demand_ref, acc_ref)
    acc_ref[...] = shifted
    base = column_base(shifted)
    x_mid = (core * HALF).astype(jnp.float32) + 0.5 * HALF
    dx = lax.broadcasted_iota(jnp.int32, (1, HALF), 1).astype(jnp.float32) - 0.5 * (HALF - 1)
    dy = lax.broadcasted_iota(jnp.int32, (TSIDE, 1), 0).astype(jnp.float32) - 0.5 * (TSIDE - 1)
    for slot, out_ref in ((0, keep_ref), (1, send_ref)):
        y_mid = ((me ^ slot) * TSIDE).astype(jnp.float32) + 0.5 * TSIDE
        lift = (dx * (dx + 2.0 * (x_mid - MIDDLE)) + dy * (dy + 2.0 * (y_mid - MIDDLE))) * SCALE
        out_ref[:TSIDE, :] = swap_half(acc_ref[:, slot, :] + lift)
        part = column_part(factors, mask_ref, base, slot)
        cap = cap_ref[slot : slot + 1, :]
        pieces = [part[:, :HALF], part[:, HALF:], cap[:, :HALF], cap[:, HALF:]]
        pieces += [jnp.zeros((TAIL - ROW_MASK, HALF), jnp.float32)]
        out_ref[TSIDE:, :] = jnp.concatenate(pieces, axis=0)


def exchange(block, distance):
    devices = lax.axis_size("tile")
    return lax.ppermute(block, "tile", [(i, i ^ distance) for i in range(devices)])


def on_device_all_rows(log_demand, log_capacity, warm_potential, facility_xy, pair_block, pair_count):
    slots = lax.axis_size("tile")
    width = log_capacity.shape[1]
    light = pltpu.CompilerParams(vmem_limit_bytes=4 * 1024 * 1024)
    heavy = pltpu.CompilerParams(vmem_limit_bytes=16 * 1024 * 1024)
    local = (log_demand, log_capacity, warm_potential, pair_block, pair_count.reshape(1, -1))
    local = [pltpu.with_memory_space_constraint(x, pltpu.HBM) for x in local]
    message = pl.pallas_call(
        pack_kernel,
        in_specs=[pl.BlockSpec(memory_space=pltpu.HBM)] * len(local),
        out_shape=jax.ShapeDtypeStruct((ROWS, HALF), jnp.float32),
        scratch_shapes=[pltpu.VMEM(x.shape, x.dtype) for x in local]
        + [pltpu.SemaphoreType.DMA((len(local),))],
        compiler_params=light,
        name="pack",
    )(*local)
    factors = pl.pallas_call(
        lambda *refs: setup_kernel(slots, *refs),
        out_shape=(
            jax.ShapeDtypeStruct((slots, 2 * HALF, width), jnp.bfloat16),
            jax.ShapeDtypeStruct((slots, TSIDE, SUBLANES, width), jnp.float32),
            jax.ShapeDtypeStruct((slots, slots, width), jnp.float32),
        ),
        compiler_params=light,
        name="setup",
    )(facility_xy)
    lines = message[None]
    distance = STEP
    while distance < slots:
        lines = jnp.concatenate([lines, exchange(lines, distance)], axis=0)
        distance *= 2
    same = lines[:, :KEEP_ROWS]
    across = lines[:, TSIDE:]
    gathered = (lines, exchange(across, 1), exchange(same, 2), exchange(across, 3))
    early = pl.pallas_call(
        early_kernel,
        out_shape=jax.ShapeDtypeStruct((slots // STEP, TSIDE, slots, HALF), jnp.float32),
        compiler_params=heavy,
        name="early",
    )(lines, *factors)
    part, mask, demand, cap = pl.pallas_call(
        first_kernel,
        out_shape=(
            jax.ShapeDtypeStruct((slots, width), jnp.float32),
            jax.ShapeDtypeStruct((slots, slots, HALF), jnp.float32),
            jax.ShapeDtypeStruct((TSIDE, slots, HALF), jnp.float32),
            jax.ShapeDtypeStruct((slots, width), jnp.float32),
        ),
        scratch_shapes=[pltpu.VMEM((TSIDE, slots, HALF), jnp.float32)],
        compiler_params=heavy,
        name="first_iteration",
    )(*gathered, *factors, early)
    other = exchange(part, 1)
    keep, send = pl.pallas_call(
        second_kernel,
        out_shape=(
            jax.ShapeDtypeStruct((KEEP_ROWS, HALF), jnp.float32),
            jax.ShapeDtypeStruct((KEEP_ROWS, HALF), jnp.float32),
        ),
        scratch_shapes=[
            pltpu.VMEM((slots, width), jnp.float32),
            pltpu.VMEM((TSIDE, slots, HALF), jnp.float32),
        ],
        compiler_params=heavy,
        name="second_iteration",
    )(*factors, mask, demand, cap, part, other)
    got = exchange(send, 1)
    return pl.pallas_call(
        unpack_kernel,
        out_shape=(
            jax.ShapeDtypeStruct(log_demand.shape, jnp.float32),
            jax.ShapeDtypeStruct(log_capacity.shape, jnp.float32),
        ),
        compiler_params=light,
        name="unpack",
    )(keep, got)


def from_behind(block, axis, distance):
    devices = range(lax.axis_size(axis))
    route = [(i - distance, i) for i in devices if i - distance in devices]
    return lax.ppermute(block, axis, route)


def cell_coords(tile_index):
    cell_ids = jnp.arange(TSIDE * TSIDE, dtype=jnp.int32)
    column = tile_index % TILE_COLS * TSIDE + cell_ids % TSIDE
    row_cell = tile_index // TILE_COLS * TSIDE + cell_ids // TSIDE
    return (column.astype(jnp.float32) + 0.5, row_cell.astype(jnp.float32) + 0.5)


def pair_cost(coord_x, coord_y, positions):
    delta_x = coord_x[None, :, None] - positions[:, 0, :][:, None, :]
    delta_y = coord_y[None, :, None] - positions[:, 1, :][:, None, :]
    return (delta_x * delta_x + delta_y * delta_y) / float(REACH * REACH)


def tile_pass(tile_index, demand_row, potentials, positions, active):
    coord_x, coord_y = cell_coords(tile_index)
    pair_costs = pair_cost(coord_x, coord_y, positions)
    scores = jnp.where(active[:, None, None], potentials[:, None, :] - pair_costs, LOWEST)
    row_top = jnp.max(scores, axis=(0, 2))
    row_sum = jnp.sum(jnp.exp(scores - row_top[None, :, None]), axis=(0, 2))
    cell_pot = demand_row - (row_top + jnp.log(row_sum))
    column_scores = cell_pot[None, :, None] - pair_costs
    col_top = jnp.max(column_scores, axis=1)
    col_sum = jnp.sum(jnp.exp(column_scores - col_top[:, None, :]), axis=1)
    col_top = jnp.where(active[:, None], col_top, LOWEST)
    col_sum = jnp.where(active[:, None], col_sum, 0.0)
    return (cell_pot, col_top, col_sum)


def merge_parts(top_a, sum_a, top_b, sum_b):
    top_new = jnp.maximum(top_a, top_b)
    return (top_new, sum_a * jnp.exp(top_a - top_new) + sum_b * jnp.exp(top_b - top_new))


def on_device(log_demand, log_capacity, warm_potential, facility_xy, pair_block, pair_count):
    tiles_here = log_demand.shape[0]
    blocks_here = log_capacity.shape[0]
    block_width = log_capacity.shape[1]
    devices_along = lax.axis_size("tile")
    my_index = lax.axis_index("tile")
    reach = min(devices_along - 1, (SPAN + blocks_here - 1) // blocks_here)
    window = 2 * reach + 1
    tile_ids = my_index * tiles_here + jnp.arange(tiles_here, dtype=jnp.int32)
    slot_ids = jnp.arange(KSLOTS, dtype=jnp.int32)
    first_block = (my_index - reach) * blocks_here
    local_block = pair_block - first_block
    facility_pot = warm_potential
    cell_pot = log_demand
    for step_index in range(ITERS):
        slabs = []
        for position in range(window):
            distance = reach - position
            if distance == 0:
                slabs.append(facility_pot)
            else:
                slabs.append(from_behind(facility_pot, "tile", distance))
        window_pot = jnp.concatenate(slabs, axis=0)

        def one_tile(inputs):
            tile_index, demand_row, blocks, nearby, slot_limit = inputs
            active = slot_ids < slot_limit
            return tile_pass(
                tile_index, demand_row, window_pot[nearby], facility_xy[blocks], active
            )

        cell_pot, col_top, col_sum = lax.map(
            one_tile, (tile_ids, log_demand, pair_block, local_block, pair_count)
        )
        flat_ids = local_block.reshape(-1)
        flat_top = col_top.reshape(-1, block_width)
        flat_sum = col_sum.reshape(-1, block_width)
        local_top = (
            jnp.full((window * blocks_here, block_width), LOWEST, jnp.float32)
            .at[flat_ids]
            .max(flat_top)
        )
        local_sum = (
            jnp.zeros((window * blocks_here, block_width), jnp.float32)
            .at[flat_ids]
            .add(flat_sum * jnp.exp(flat_top - local_top[flat_ids]))
        )

        def slab_of(position):
            return (
                local_top[position * blocks_here : (position + 1) * blocks_here],
                local_sum[position * blocks_here : (position + 1) * blocks_here],
            )

        own_top, block_sum = slab_of(reach)
        for distance in range(-reach, reach + 1):
            if distance != 0:
                send_top, send_sum = slab_of(reach + distance)
                got_top, got_sum = from_behind((send_top, send_sum), "tile", distance)
                source = my_index - distance
                valid = (source >= 0) & (source < devices_along)
                got_top = jnp.where(valid, got_top, LOWEST)
                got_sum = jnp.where(valid, got_sum, 0.0)
                own_top, block_sum = merge_parts(own_top, block_sum, got_top, got_sum)
        facility_pot = log_capacity - (own_top + jnp.log(block_sum))
    return (cell_pot, facility_pot)


def solution(mesh):
    placed = (
        P(("groups", "tile"), None),
        P(("groups", "tile"), None),
        P(("groups", "tile"), None),
        P("groups", None, None),
        P(("groups", "tile"), None),
        P(("groups", "tile")),
    )
    devices = mesh.shape["tile"]
    small = devices % 2 == 0 and devices * COLS_HALF == HALF

    def program(log_demand, log_capacity, warm_potential, facility_xy, pair_block, pair_count):
        one_row = log_demand.shape[0] == mesh.size * TILE_COLS and log_capacity.shape[0] == mesh.size
        fits = small and one_row and log_capacity.shape[1] == 2 * HALF
        body = on_device_all_rows if fits else on_device
        return jax.shard_map(
            body,
            mesh=mesh,
            in_specs=placed,
            out_specs=(P(("groups", "tile"), None), P(("groups", "tile"), None)),
            check_vma=False,
        )(log_demand, log_capacity, warm_potential, facility_xy, pair_block, pair_count)

    return program
```

```python
import jax
import jax.numpy as jnp
from jax import lax
from jax.experimental import pallas as pl
from jax.experimental.pallas import tpu as pltpu
from jax.sharding import PartitionSpec as P

TSIDE = 16
TILE_COLS = 16
KSLOTS = 16
ITERS = 2
REACH = 64
SPAN = 16


LOWEST = -1e30

HALF = TSIDE * TILE_COLS // 2
COLS_HALF = TILE_COLS // 2
SCALE = 1.0 / float(REACH * REACH)
MIDDLE = 736.0
TAIL = 8
ROWS = 2 * TSIDE + TAIL
KEEP_ROWS = TSIDE + TAIL
ROW_POT = 0
ROW_CAP = 2
ROW_MASK = 4
STEP = 4
SUBLANES = 8
LOG2E = 1.4426950408889634
LN2 = 0.6931471805599453


def dot_nt(a, b):
    return lax.dot_general(a, b, (((1,), (1,)), ((), ())), preferred_element_type=jnp.float32)


def dot_nn(a, b):
    return lax.dot_general(a, b, (((1,), (0,)), ((), ())), preferred_element_type=jnp.float32)


def split(values):
    high = values.astype(jnp.bfloat16)
    low = (values - high.astype(jnp.float32)).astype(jnp.bfloat16)
    return high, low


def halves_of(row_pair):
    return jnp.concatenate([row_pair[0:1, :], row_pair[1:2, :]], axis=1)


class Gathered:
    def __init__(self, refs):
        self.refs = refs
        self.slots = range(len(refs) * refs[0].shape[0])

    def block_of(self, slot, first, rows):
        return self.refs[slot % STEP][slot // STEP, first : first + rows, :]

    def demand(self, slot):
        return self.block_of(slot, TAIL if slot % 2 else 0, TSIDE)

    def tail(self, slot):
        return self.block_of(slot, 0 if slot % 2 else TSIDE, TAIL)

    def potential(self, slot):
        return halves_of(self.tail(slot)[ROW_POT : ROW_POT + 2])

    def capacity(self, slot):
        return halves_of(self.tail(slot)[ROW_CAP : ROW_CAP + 2])

    def mask(self, slot):
        row = ROW_MASK + slot % 2
        return self.tail(slot)[row : row + 1]


def setup_kernel(slots, xy_ref, xf_ref, yf_ref, cost_ref):
    me = lax.axis_index("tile")
    x_mid = (me % 2 * HALF).astype(jnp.float32) + 0.5 * HALF
    row_ids = me ^ lax.broadcasted_iota(jnp.int32, (slots, 1), 0)
    y_mid = (row_ids * TSIDE).astype(jnp.float32) + 0.5 * TSIDE
    x_off = lax.broadcasted_iota(jnp.int32, (HALF, 1), 0).astype(jnp.float32) - 0.5 * (HALF - 1)
    y_off = lax.broadcasted_iota(jnp.int32, (TSIDE, 1), 0).astype(jnp.float32) - 0.5 * (TSIDE - 1)
    for slot in range(slots):
        block = me ^ slot
        fx = xy_ref[block, 0:1, :]
        fy = xy_ref[block, 1:2, :]
        high, low = split(jnp.exp(x_off * ((fx - MIDDLE) * (2.0 * SCALE))))
        xf_ref[slot, :HALF, :] = high
        xf_ref[slot, HALF:, :] = low
        y_factor = jnp.exp(y_off * ((fy - MIDDLE) * (2.0 * SCALE)))
        yf_ref[slot] = jnp.broadcast_to(y_factor[:, None, :], yf_ref.shape[1:])
        dx = x_mid - fx
        dy = y_mid - fy
        cost_ref[slot] = (dx * dx + dy * dy) * SCALE


def build_mask(gathered, me, mask_ref):
    slots = len(gathered.slots)
    marks = jnp.concatenate([gathered.mask(slot) for slot in gathered.slots], axis=0)
    lane_block = lax.broadcasted_iota(jnp.int32, (slots, slots, HALF), 2) // COLS_HALF
    own_block = lax.broadcasted_iota(jnp.int32, (slots, slots, HALF), 0) ^ me
    picked = jnp.where(lane_block == own_block, marks[None], 0.0)
    picked = picked.reshape(slots * slots, HALF).astype(jnp.bfloat16)
    source = lax.broadcasted_iota(jnp.int32, (HALF, HALF), 0) % COLS_HALF
    target = lax.broadcasted_iota(jnp.int32, (HALF, HALF), 1) // TSIDE
    spread = jnp.where(source == target, 1.0, 0.0).astype(jnp.bfloat16)
    mask_ref[...] = dot_nn(picked, spread).reshape(slots, slots, HALF)


def block_top(potential, factors, slot):
    return jnp.max(potential(slot) - factors[2][slot], axis=1, keepdims=True)


def block_sums(potential, factors, top, slot):
    xf_ref, yf_ref, cost_ref = factors
    slots = top.shape[0]
    weight = jnp.exp(potential(slot) - cost_ref[slot] - top)
    parts = [weight[i : i + SUBLANES][None] * yf_ref[slot] for i in range(0, slots, SUBLANES)]
    lhs = jnp.concatenate(parts, axis=1)
    a_high, a_low = split(lhs.reshape(TSIDE * slots, lhs.shape[-1]))
    return row_product(a_high, a_low, xf_ref, slot).reshape(TSIDE, slots, HALF)


def row_pass(potential, factors, mask_ref, demand_ref, acc_ref, early_ref=None):
    slots = mask_ref.shape[0]
    best = jnp.full((slots, HALF), LOWEST, jnp.float32)
    tops = []
    for slot in range(slots):
        top = block_top(potential, factors, slot)
        tops.append(top)
        best = jnp.maximum(best, jnp.where(mask_ref[slot] > 0.0, top, LOWEST))
    for slot in range(slots):
        top = tops[slot]
        if early_ref is not None and slot % STEP == 0:
            part = early_ref[slot // STEP]
        else:
            part = block_sums(potential, factors, top, slot)
        scale = jnp.where(mask_ref[slot] > 0.0, jnp.exp(jnp.minimum(top - best, 0.0)), 0.0)
        scaled = part * scale[None]
        if slot == 0:
            acc_ref[...] = scaled
        else:
            acc_ref[...] += scaled
    return demand_ref[...] - best[None] - jnp.log(acc_ref[...])


def row_product(a_high, a_low, xf_ref, slot):
    both = dot_nt(a_high, xf_ref[slot])
    third = dot_nt(a_low, xf_ref[slot, :HALF, :])
    return both[:, :HALF] + both[:, HALF:] + third


def column_product(w_high, w_low, xf_ref, slot):
    mixed = dot_nn(jnp.concatenate([w_high, w_high], axis=1), xf_ref[slot])
    return mixed + dot_nn(w_low, xf_ref[slot, :HALF, :])


def column_base(shifted):
    scaled = shifted * LOG2E
    level = jnp.ceil(jnp.max(scaled, axis=0))
    high, low = split(jnp.exp2(scaled - level[None]))
    return level, high, low


def column_part(factors, mask_ref, base, slot):
    xf_ref, yf_ref, cost_ref = factors
    level, high, low = base
    slots = level.shape[0]
    active = mask_ref[slot] > 0.0
    top = jnp.max(jnp.where(active, level, LOWEST), axis=1, keepdims=True)
    scale = jnp.where(active, jnp.exp2(jnp.minimum(level - top, 0.0)), 0.0).astype(jnp.bfloat16)
    w_high = (high * scale[None]).reshape(TSIDE * slots, HALF)
    w_low = (low * scale[None]).reshape(TSIDE * slots, HALF)
    mixed = column_product(w_high, w_low, xf_ref, slot)
    mixed = mixed.reshape(TSIDE, slots, mixed.shape[-1])
    sums = [
        jnp.sum(mixed[:, i : i + SUBLANES] * yf_ref[slot], axis=0) for i in range(0, slots, SUBLANES)
    ]
    sums = jnp.concatenate(sums, axis=0)
    tops = top * LN2 - cost_ref[slot]
    best = jnp.max(tops, axis=0, keepdims=True)
    total = jnp.sum(sums * jnp.exp(tops - best), axis=0, keepdims=True)
    return best + jnp.log(total)


def log_add(a, b):
    top = jnp.maximum(a, b)
    return top + jnp.log(jnp.exp(a - top) + jnp.exp(b - top))


def swap_minor(values):
    lane_group = lax.broadcasted_iota(jnp.int32, (TSIDE, HALF), 1) // TSIDE
    diagonal = lane_group[:COLS_HALF] == lax.broadcasted_iota(jnp.int32, (COLS_HALF, HALF), 0)
    result = []
    for b in range(TSIDE):
        start = b // COLS_HALF * HALF
        piece = jnp.where(lane_group == b % COLS_HALF, values[:, start : start + HALF], 0.0)
        for shift in (TSIDE, 2 * TSIDE, 4 * TSIDE):
            piece = piece + pltpu.roll(piece, shift, 1)
        halves = [
            jnp.sum(jnp.where(diagonal, piece[start : start + COLS_HALF], 0.0), axis=0, keepdims=True)
            for start in (0, COLS_HALF)
        ]
        result.append(halves)
    return result


def swap_half(values):
    lane_group = lax.broadcasted_iota(jnp.int32, (TSIDE, HALF), 1) // TSIDE
    diagonal = lane_group[:COLS_HALF] == lax.broadcasted_iota(jnp.int32, (COLS_HALF, HALF), 0)
    result = ([], [])
    for tile in range(COLS_HALF):
        piece = jnp.where(lane_group == tile, values, 0.0)
        for shift in (TSIDE, 2 * TSIDE, 4 * TSIDE):
            piece = piece + pltpu.roll(piece, shift, 1)
        for half in (0, 1):
            part = piece[half * COLS_HALF : (half + 1) * COLS_HALF]
            result[half].append(jnp.sum(jnp.where(diagonal, part, 0.0), axis=0, keepdims=True))
    return jnp.concatenate(result[0] + result[1], axis=0)


def pack_kernel(*refs):
    sources, message_ref, targets, sems = refs[:5], refs[5], refs[6:11], refs[11]
    copies = [
        pltpu.make_async_copy(source, target, sems.at[i])
        for i, (source, target) in enumerate(zip(sources, targets, strict=True))
    ]
    for copy in copies:
        copy.start()
    for copy in copies:
        copy.wait()
    demand_ref, cap_ref, pot_ref, pair_ref, count_ref = targets
    tiles = 2 * COLS_HALF
    tile_of = lax.broadcasted_iota(jnp.int32, (tiles, tiles), 0)
    lane_of = lax.broadcasted_iota(jnp.int32, (tiles, tiles), 1)
    counts = jnp.sum(jnp.where(tile_of == lane_of, count_ref[...], 0), axis=1, keepdims=True)
    pairs = jnp.where(lax.broadcasted_iota(jnp.int32, (tiles, KSLOTS), 1) < counts, pair_ref[...], -1)
    lanes = lax.broadcasted_iota(jnp.int32, (tiles, HALF), 1)
    found = lanes < 0
    for slot in range(KSLOTS):
        found = found | (pairs[:, slot : slot + 1] == lanes // COLS_HALF)
    own = lax.broadcasted_iota(jnp.int32, (tiles, HALF), 0) % COLS_HALF == lanes % COLS_HALF
    marks = jnp.where(found & own, 1.0, 0.0)
    grid_rows = swap_minor(demand_ref[...])
    is_left = lax.axis_index("tile") % 2 == 0
    tops = [jnp.sum(marks[start : start + COLS_HALF], axis=0, keepdims=True) for start in (0, COLS_HALF)]
    sides = [jnp.concatenate([row[half] for row in grid_rows], axis=0) for half in (0, 1)]
    message_ref[:TSIDE, :] = jnp.where(is_left, sides[0], sides[1])
    message_ref[TSIDE + TAIL :, :] = jnp.where(is_left, sides[1], sides[0])
    pieces = [pot_ref[:, :HALF], pot_ref[:, HALF:], cap_ref[:, :HALF], cap_ref[:, HALF:]]
    pieces += [jnp.where(is_left, tops[0], tops[1]), jnp.where(is_left, tops[1], tops[0])]
    pieces += [jnp.zeros((TAIL - ROW_MASK - 2, HALF), jnp.float32)]
    message_ref[TSIDE : TSIDE + TAIL, :] = jnp.concatenate(pieces, axis=0)


def unpack_kernel(keep_ref, got_ref, cell_ref, fac_ref):
    core = lax.axis_index("tile") % 2
    for side, ref in ((core, keep_ref), (1 - core, got_ref)):
        rows = pl.ds(pl.multiple_of(side * COLS_HALF, COLS_HALF), COLS_HALF)
        cell_ref[rows, :HALF] = ref[:COLS_HALF, :]
        cell_ref[rows, HALF:] = ref[COLS_HALF:TSIDE, :]
    tail = keep_ref[TSIDE:, :]
    total = log_add(tail[ROW_POT : ROW_POT + 2], got_ref[TSIDE + ROW_POT : TSIDE + ROW_POT + 2, :])
    fac = tail[ROW_CAP : ROW_CAP + 2] - total
    fac_ref[:, :HALF] = fac[0:1]
    fac_ref[:, HALF:] = fac[1:2]


def early_kernel(*refs):
    gathered = Gathered(refs[:1])
    factors = refs[1:4]
    for line in range(refs[0].shape[0]):
        slot = line * STEP
        top = block_top(gathered.potential, factors, slot)
        refs[4][line] = block_sums(gathered.potential, factors, top, slot)


def first_kernel(*refs):
    gathered = Gathered(refs[:STEP])
    factors = refs[STEP : STEP + 3]
    early_ref, part_ref, mask_ref, demand_ref, cap_ref, acc_ref = refs[STEP + 3 :]
    build_mask(gathered, lax.axis_index("tile"), mask_ref)
    for slot in gathered.slots:
        demand_ref[:, slot, :] = gathered.demand(slot)
        cap_ref[slot : slot + 1, :] = gathered.capacity(slot)
    base = column_base(row_pass(gathered.potential, factors, mask_ref, demand_ref, acc_ref, early_ref))
    for slot in gathered.slots:
        part_ref[slot : slot + 1, :] = column_part(factors, mask_ref, base, slot)


def second_kernel(*refs):
    factors = refs[:3]
    mask_ref, demand_ref, cap_ref, mine_ref, other_ref, keep_ref, send_ref, pot_ref, acc_ref = refs[3:]
    me = lax.axis_index("tile")
    core = me % 2
    slots = mask_ref.shape[0]
    other = other_ref[...]
    even = lax.broadcasted_iota(jnp.int32, other.shape, 0) % 2 == 0
    swapped = jnp.where(even, pltpu.roll(other, slots - 1, 0), pltpu.roll(other, 1, 0))
    pot_ref[...] = cap_ref[...] - log_add(mine_ref[...], swapped)

    def potential(slot):
        return pot_ref[slot : slot + 1, :]

    shifted = row_pass(potential, factors, mask_ref, demand_ref, acc_ref)
    acc_ref[...] = shifted
    base = column_base(shifted)
    x_mid = (core * HALF).astype(jnp.float32) + 0.5 * HALF
    dx = lax.broadcasted_iota(jnp.int32, (1, HALF), 1).astype(jnp.float32) - 0.5 * (HALF - 1)
    dy = lax.broadcasted_iota(jnp.int32, (TSIDE, 1), 0).astype(jnp.float32) - 0.5 * (TSIDE - 1)
    for slot, out_ref in ((0, keep_ref), (1, send_ref)):
        y_mid = ((me ^ slot) * TSIDE).astype(jnp.float32) + 0.5 * TSIDE
        lift = (dx * (dx + 2.0 * (x_mid - MIDDLE)) + dy * (dy + 2.0 * (y_mid - MIDDLE))) * SCALE
        out_ref[:TSIDE, :] = swap_half(acc_ref[:, slot, :] + lift)
        part = column_part(factors, mask_ref, base, slot)
        cap = cap_ref[slot : slot + 1, :]
        pieces = [part[:, :HALF], part[:, HALF:], cap[:, :HALF], cap[:, HALF:]]
        pieces += [jnp.zeros((TAIL - ROW_MASK, HALF), jnp.float32)]
        out_ref[TSIDE:, :] = jnp.concatenate(pieces, axis=0)


def exchange(block, distance):
    devices = lax.axis_size("tile")
    return lax.ppermute(block, "tile", [(i, i ^ distance) for i in range(devices)])


def on_device_all_rows(log_demand, log_capacity, warm_potential, facility_xy, pair_block, pair_count):
    slots = lax.axis_size("tile")
    width = log_capacity.shape[1]
    light = pltpu.CompilerParams(vmem_limit_bytes=4 * 1024 * 1024)
    heavy = pltpu.CompilerParams(vmem_limit_bytes=16 * 1024 * 1024)
    local = (log_demand, log_capacity, warm_potential, pair_block, pair_count.reshape(1, -1))
    local = [pltpu.with_memory_space_constraint(x, pltpu.HBM) for x in local]
    message = pl.pallas_call(
        pack_kernel,
        in_specs=[pl.BlockSpec(memory_space=pltpu.HBM)] * len(local),
        out_shape=jax.ShapeDtypeStruct((ROWS, HALF), jnp.float32),
        scratch_shapes=[pltpu.VMEM(x.shape, x.dtype) for x in local]
        + [pltpu.SemaphoreType.DMA((len(local),))],
        compiler_params=light,
        name="pack",
    )(*local)
    factors = pl.pallas_call(
        lambda *refs: setup_kernel(slots, *refs),
        out_shape=(
            jax.ShapeDtypeStruct((slots, 2 * HALF, width), jnp.bfloat16),
            jax.ShapeDtypeStruct((slots, TSIDE, SUBLANES, width), jnp.float32),
            jax.ShapeDtypeStruct((slots, slots, width), jnp.float32),
        ),
        compiler_params=light,
        name="setup",
    )(facility_xy)
    lines = message[None]
    lines = jnp.concatenate([lines] + [exchange(lines, STEP * i) for i in range(1, slots // STEP)], axis=0)
    same = lines[:, :KEEP_ROWS]
    across = lines[:, TSIDE:]
    gathered = (lines, exchange(across, 1), exchange(same, 2), exchange(across, 3))
    early = pl.pallas_call(
        early_kernel,
        out_shape=jax.ShapeDtypeStruct((slots // STEP, TSIDE, slots, HALF), jnp.float32),
        compiler_params=heavy,
        name="early",
    )(lines, *factors)
    part, mask, demand, cap = pl.pallas_call(
        first_kernel,
        out_shape=(
            jax.ShapeDtypeStruct((slots, width), jnp.float32),
            jax.ShapeDtypeStruct((slots, slots, HALF), jnp.float32),
            jax.ShapeDtypeStruct((TSIDE, slots, HALF), jnp.float32),
            jax.ShapeDtypeStruct((slots, width), jnp.float32),
        ),
        scratch_shapes=[pltpu.VMEM((TSIDE, slots, HALF), jnp.float32)],
        compiler_params=heavy,
        name="first_iteration",
    )(*gathered, *factors, early)
    other = exchange(part, 1)
    keep, send = pl.pallas_call(
        second_kernel,
        out_shape=(
            jax.ShapeDtypeStruct((KEEP_ROWS, HALF), jnp.float32),
            jax.ShapeDtypeStruct((KEEP_ROWS, HALF), jnp.float32),
        ),
        scratch_shapes=[
            pltpu.VMEM((slots, width), jnp.float32),
            pltpu.VMEM((TSIDE, slots, HALF), jnp.float32),
        ],
        compiler_params=heavy,
        name="second_iteration",
    )(*factors, mask, demand, cap, part, other)
    got = exchange(send, 1)
    return pl.pallas_call(
        unpack_kernel,
        out_shape=(
            jax.ShapeDtypeStruct(log_demand.shape, jnp.float32),
            jax.ShapeDtypeStruct(log_capacity.shape, jnp.float32),
        ),
        compiler_params=light,
        name="unpack",
    )(keep, got)


def from_behind(block, axis, distance):
    devices = range(lax.axis_size(axis))
    route = [(i - distance, i) for i in devices if i - distance in devices]
    return lax.ppermute(block, axis, route)


def cell_coords(tile_index):
    cell_ids = jnp.arange(TSIDE * TSIDE, dtype=jnp.int32)
    column = tile_index % TILE_COLS * TSIDE + cell_ids % TSIDE
    row_cell = tile_index // TILE_COLS * TSIDE + cell_ids // TSIDE
    return (column.astype(jnp.float32) + 0.5, row_cell.astype(jnp.float32) + 0.5)


def pair_cost(coord_x, coord_y, positions):
    delta_x = coord_x[None, :, None] - positions[:, 0, :][:, None, :]
    delta_y = coord_y[None, :, None] - positions[:, 1, :][:, None, :]
    return (delta_x * delta_x + delta_y * delta_y) / float(REACH * REACH)


def tile_pass(tile_index, demand_row, potentials, positions, active):
    coord_x, coord_y = cell_coords(tile_index)
    pair_costs = pair_cost(coord_x, coord_y, positions)
    scores = jnp.where(active[:, None, None], potentials[:, None, :] - pair_costs, LOWEST)
    row_top = jnp.max(scores, axis=(0, 2))
    row_sum = jnp.sum(jnp.exp(scores - row_top[None, :, None]), axis=(0, 2))
    cell_pot = demand_row - (row_top + jnp.log(row_sum))
    column_scores = cell_pot[None, :, None] - pair_costs
    col_top = jnp.max(column_scores, axis=1)
    col_sum = jnp.sum(jnp.exp(column_scores - col_top[:, None, :]), axis=1)
    col_top = jnp.where(active[:, None], col_top, LOWEST)
    col_sum = jnp.where(active[:, None], col_sum, 0.0)
    return (cell_pot, col_top, col_sum)


def merge_parts(top_a, sum_a, top_b, sum_b):
    top_new = jnp.maximum(top_a, top_b)
    return (top_new, sum_a * jnp.exp(top_a - top_new) + sum_b * jnp.exp(top_b - top_new))


def on_device(log_demand, log_capacity, warm_potential, facility_xy, pair_block, pair_count):
    tiles_here = log_demand.shape[0]
    blocks_here = log_capacity.shape[0]
    block_width = log_capacity.shape[1]
    devices_along = lax.axis_size("tile")
    my_index = lax.axis_index("tile")
    reach = min(devices_along - 1, (SPAN + blocks_here - 1) // blocks_here)
    window = 2 * reach + 1
    tile_ids = my_index * tiles_here + jnp.arange(tiles_here, dtype=jnp.int32)
    slot_ids = jnp.arange(KSLOTS, dtype=jnp.int32)
    first_block = (my_index - reach) * blocks_here
    local_block = pair_block - first_block
    facility_pot = warm_potential
    cell_pot = log_demand
    for step_index in range(ITERS):
        slabs = []
        for position in range(window):
            distance = reach - position
            if distance == 0:
                slabs.append(facility_pot)
            else:
                slabs.append(from_behind(facility_pot, "tile", distance))
        window_pot = jnp.concatenate(slabs, axis=0)

        def one_tile(inputs):
            tile_index, demand_row, blocks, nearby, slot_limit = inputs
            active = slot_ids < slot_limit
            return tile_pass(
                tile_index, demand_row, window_pot[nearby], facility_xy[blocks], active
            )

        cell_pot, col_top, col_sum = lax.map(
            one_tile, (tile_ids, log_demand, pair_block, local_block, pair_count)
        )
        flat_ids = local_block.reshape(-1)
        flat_top = col_top.reshape(-1, block_width)
        flat_sum = col_sum.reshape(-1, block_width)
        local_top = (
            jnp.full((window * blocks_here, block_width), LOWEST, jnp.float32)
            .at[flat_ids]
            .max(flat_top)
        )
        local_sum = (
            jnp.zeros((window * blocks_here, block_width), jnp.float32)
            .at[flat_ids]
            .add(flat_sum * jnp.exp(flat_top - local_top[flat_ids]))
        )

        def slab_of(position):
            return (
                local_top[position * blocks_here : (position + 1) * blocks_here],
                local_sum[position * blocks_here : (position + 1) * blocks_here],
            )

        own_top, block_sum = slab_of(reach)
        for distance in range(-reach, reach + 1):
            if distance != 0:
                send_top, send_sum = slab_of(reach + distance)
                got_top, got_sum = from_behind((send_top, send_sum), "tile", distance)
                source = my_index - distance
                valid = (source >= 0) & (source < devices_along)
                got_top = jnp.where(valid, got_top, LOWEST)
                got_sum = jnp.where(valid, got_sum, 0.0)
                own_top, block_sum = merge_parts(own_top, block_sum, got_top, got_sum)
        facility_pot = log_capacity - (own_top + jnp.log(block_sum))
    return (cell_pot, facility_pot)


def solution(mesh):
    placed = (
        P(("groups", "tile"), None),
        P(("groups", "tile"), None),
        P(("groups", "tile"), None),
        P("groups", None, None),
        P(("groups", "tile"), None),
        P(("groups", "tile")),
    )
    devices = mesh.shape["tile"]
    small = devices % 2 == 0 and devices * COLS_HALF == HALF

    def program(log_demand, log_capacity, warm_potential, facility_xy, pair_block, pair_count):
        one_row = log_demand.shape[0] == mesh.size * TILE_COLS and log_capacity.shape[0] == mesh.size
        fits = small and one_row and log_capacity.shape[1] == 2 * HALF
        body = on_device_all_rows if fits else on_device
        return jax.shard_map(
            body,
            mesh=mesh,
            in_specs=placed,
            out_specs=(P(("groups", "tile"), None), P(("groups", "tile"), None)),
            check_vma=False,
        )(log_demand, log_capacity, warm_potential, facility_xy, pair_block, pair_count)

    return program
```

```python
import jax
import jax.numpy as jnp
from jax import lax
from jax.experimental import pallas as pl
from jax.experimental.pallas import tpu as pltpu
from jax.sharding import PartitionSpec as P

TSIDE = 16
TILE_COLS = 16
KSLOTS = 16
ITERS = 2
REACH = 64
SPAN = 16


LOWEST = -1e30

HALF = TSIDE * TILE_COLS // 2
COLS_HALF = TILE_COLS // 2
SCALE = 1.0 / float(REACH * REACH)
MIDDLE = 736.0
TAIL = 8
ROWS = 2 * TSIDE + TAIL
KEEP_ROWS = TSIDE + TAIL
ROW_POT = 0
ROW_CAP = 2
ROW_MASK = 4
STEP = 4
EARLY = 3
SUBLANES = 8
LOG2E = 1.4426950408889634
LN2 = 0.6931471805599453


def dot_nt(a, b):
    return lax.dot_general(a, b, (((1,), (1,)), ((), ())), preferred_element_type=jnp.float32)


def dot_nn(a, b):
    return lax.dot_general(a, b, (((1,), (0,)), ((), ())), preferred_element_type=jnp.float32)


def split(values):
    high = values.astype(jnp.bfloat16)
    low = (values - high.astype(jnp.float32)).astype(jnp.bfloat16)
    return high, low


def halves_of(row_pair):
    return jnp.concatenate([row_pair[0:1, :], row_pair[1:2, :]], axis=1)


class Gathered:
    def __init__(self, refs):
        self.refs = refs
        self.slots = range(len(refs) * refs[0].shape[0])

    def block_of(self, slot, first, rows):
        return self.refs[slot % STEP][slot // STEP, first : first + rows, :]

    def demand(self, slot):
        return self.block_of(slot, TAIL if slot % 2 else 0, TSIDE)

    def tail(self, slot):
        return self.block_of(slot, 0 if slot % 2 else TSIDE, TAIL)

    def potential(self, slot):
        return halves_of(self.tail(slot)[ROW_POT : ROW_POT + 2])

    def capacity(self, slot):
        return halves_of(self.tail(slot)[ROW_CAP : ROW_CAP + 2])

    def mask(self, slot):
        row = ROW_MASK + slot % 2
        return self.tail(slot)[row : row + 1]


def setup_kernel(slots, xy_ref, xf_ref, yf_ref, cost_ref):
    me = lax.axis_index("tile")
    x_mid = (me % 2 * HALF).astype(jnp.float32) + 0.5 * HALF
    row_ids = me ^ lax.broadcasted_iota(jnp.int32, (slots, 1), 0)
    y_mid = (row_ids * TSIDE).astype(jnp.float32) + 0.5 * TSIDE
    x_off = lax.broadcasted_iota(jnp.int32, (HALF, 1), 0).astype(jnp.float32) - 0.5 * (HALF - 1)
    y_off = lax.broadcasted_iota(jnp.int32, (TSIDE, 1), 0).astype(jnp.float32) - 0.5 * (TSIDE - 1)
    for slot in range(slots):
        block = me ^ slot
        fx = xy_ref[block, 0:1, :]
        fy = xy_ref[block, 1:2, :]
        high, low = split(jnp.exp(x_off * ((fx - MIDDLE) * (2.0 * SCALE))))
        xf_ref[slot, :HALF, :] = high
        xf_ref[slot, HALF:, :] = low
        y_factor = jnp.exp(y_off * ((fy - MIDDLE) * (2.0 * SCALE)))
        yf_ref[slot] = jnp.broadcast_to(y_factor[:, None, :], yf_ref.shape[1:])
        dx = x_mid - fx
        dy = y_mid - fy
        cost_ref[slot] = (dx * dx + dy * dy) * SCALE


def build_mask(gathered, me, mask_ref):
    slots = len(gathered.slots)
    marks = jnp.concatenate([gathered.mask(slot) for slot in gathered.slots], axis=0)
    lane_block = lax.broadcasted_iota(jnp.int32, (slots, slots, HALF), 2) // COLS_HALF
    own_block = lax.broadcasted_iota(jnp.int32, (slots, slots, HALF), 0) ^ me
    picked = jnp.where(lane_block == own_block, marks[None], 0.0)
    picked = picked.reshape(slots * slots, HALF).astype(jnp.bfloat16)
    source = lax.broadcasted_iota(jnp.int32, (HALF, HALF), 0) % COLS_HALF
    target = lax.broadcasted_iota(jnp.int32, (HALF, HALF), 1) // TSIDE
    spread = jnp.where(source == target, 1.0, 0.0).astype(jnp.bfloat16)
    mask_ref[...] = dot_nn(picked, spread).reshape(slots, slots, HALF)


def block_top(potential, factors, slot):
    return jnp.max(potential(slot) - factors[2][slot], axis=1, keepdims=True)


def block_sums(potential, factors, top, slot):
    xf_ref, yf_ref, cost_ref = factors
    slots = top.shape[0]
    weight = jnp.exp(potential(slot) - cost_ref[slot] - top)
    parts = [weight[i : i + SUBLANES][None] * yf_ref[slot] for i in range(0, slots, SUBLANES)]
    lhs = jnp.concatenate(parts, axis=1)
    a_high, a_low = split(lhs.reshape(TSIDE * slots, lhs.shape[-1]))
    return row_product(a_high, a_low, xf_ref, slot).reshape(TSIDE, slots, HALF)


def row_pass(potential, factors, mask_ref, demand_ref, acc_ref, early_refs=()):
    slots = mask_ref.shape[0]
    best = jnp.full((slots, HALF), LOWEST, jnp.float32)
    tops = []
    for slot in range(slots):
        top = block_top(potential, factors, slot)
        tops.append(top)
        best = jnp.maximum(best, jnp.where(mask_ref[slot] > 0.0, top, LOWEST))
    for slot in range(slots):
        top = tops[slot]
        if slot % STEP < len(early_refs):
            part = early_refs[slot % STEP][slot // STEP]
        else:
            part = block_sums(potential, factors, top, slot)
        scale = jnp.where(mask_ref[slot] > 0.0, jnp.exp(jnp.minimum(top - best, 0.0)), 0.0)
        scaled = part * scale[None]
        if slot == 0:
            acc_ref[...] = scaled
        else:
            acc_ref[...] += scaled
    return demand_ref[...] - best[None] - jnp.log(acc_ref[...])


def row_product(a_high, a_low, xf_ref, slot):
    both = dot_nt(a_high, xf_ref[slot])
    third = dot_nt(a_low, xf_ref[slot, :HALF, :])
    return both[:, :HALF] + both[:, HALF:] + third


def column_product(w_high, w_low, xf_ref, slot):
    mixed = dot_nn(jnp.concatenate([w_high, w_high], axis=1), xf_ref[slot])
    return mixed + dot_nn(w_low, xf_ref[slot, :HALF, :])


def column_base(shifted):
    scaled = shifted * LOG2E
    level = jnp.ceil(jnp.max(scaled, axis=0))
    high, low = split(jnp.exp2(scaled - level[None]))
    return level, high, low


def column_part(factors, mask_ref, base, slot):
    xf_ref, yf_ref, cost_ref = factors
    level, high, low = base
    slots = level.shape[0]
    active = mask_ref[slot] > 0.0
    top = jnp.max(jnp.where(active, level, LOWEST), axis=1, keepdims=True)
    scale = jnp.where(active, jnp.exp2(jnp.minimum(level - top, 0.0)), 0.0).astype(jnp.bfloat16)
    w_high = (high * scale[None]).reshape(TSIDE * slots, HALF)
    w_low = (low * scale[None]).reshape(TSIDE * slots, HALF)
    mixed = column_product(w_high, w_low, xf_ref, slot)
    mixed = mixed.reshape(TSIDE, slots, mixed.shape[-1])
    sums = [
        jnp.sum(mixed[:, i : i + SUBLANES] * yf_ref[slot], axis=0) for i in range(0, slots, SUBLANES)
    ]
    sums = jnp.concatenate(sums, axis=0)
    tops = top * LN2 - cost_ref[slot]
    best = jnp.max(tops, axis=0, keepdims=True)
    total = jnp.sum(sums * jnp.exp(tops - best), axis=0, keepdims=True)
    return best + jnp.log(total)


def log_add(a, b):
    top = jnp.maximum(a, b)
    return top + jnp.log(jnp.exp(a - top) + jnp.exp(b - top))


def swap_tile(values):
    row = lax.broadcasted_iota(jnp.int32, (COLS_HALF, HALF), 0)
    group = lax.broadcasted_iota(jnp.int32, (COLS_HALF, HALF), 1) // TSIDE
    step = 1
    while step < COLS_HALF:
        from_below = pltpu.roll(pltpu.roll(values, COLS_HALF - step, 0), TSIDE * step, 1)
        from_above = pltpu.roll(pltpu.roll(values, step, 0), HALF - TSIDE * step, 1)
        moved = jnp.where((group & step) != 0, from_below, from_above)
        values = jnp.where((row & step) == (group & step), values, moved)
        step *= 2
    return values


def pack_kernel(*refs):
    sources, message_ref, targets, sems = refs[:5], refs[5], refs[6:11], refs[11]
    copies = [
        pltpu.make_async_copy(source, target, sems.at[i])
        for i, (source, target) in enumerate(zip(sources, targets, strict=True))
    ]
    for copy in copies:
        copy.start()
    for copy in copies:
        copy.wait()
    demand_ref, cap_ref, pot_ref, pair_ref, count_ref = targets
    tiles = 2 * COLS_HALF
    tile_of = lax.broadcasted_iota(jnp.int32, (tiles, tiles), 0)
    lane_of = lax.broadcasted_iota(jnp.int32, (tiles, tiles), 1)
    counts = jnp.sum(jnp.where(tile_of == lane_of, count_ref[...], 0), axis=1, keepdims=True)
    pairs = jnp.where(lax.broadcasted_iota(jnp.int32, (tiles, KSLOTS), 1) < counts, pair_ref[...], -1)
    lanes = lax.broadcasted_iota(jnp.int32, (tiles, HALF), 1)
    found = lanes < 0
    for slot in range(KSLOTS):
        found = found | (pairs[:, slot : slot + 1] == lanes // COLS_HALF)
    own = lax.broadcasted_iota(jnp.int32, (tiles, HALF), 0) % COLS_HALF == lanes % COLS_HALF
    marks = jnp.where(found & own, 1.0, 0.0)
    is_left = lax.axis_index("tile") % 2 == 0
    tops = [jnp.sum(marks[start : start + COLS_HALF], axis=0, keepdims=True) for start in (0, COLS_HALF)]
    for start in (0, COLS_HALF):
        lanes_of = slice(start // COLS_HALF * HALF, (start // COLS_HALF + 1) * HALF)
        sides = [swap_tile(demand_ref[i : i + COLS_HALF, lanes_of]) for i in (0, COLS_HALF)]
        message_ref[start : start + COLS_HALF, :] = jnp.where(is_left, sides[0], sides[1])
        below = KEEP_ROWS + start
        message_ref[below : below + COLS_HALF, :] = jnp.where(is_left, sides[1], sides[0])
    pieces = [pot_ref[:, :HALF], pot_ref[:, HALF:], cap_ref[:, :HALF], cap_ref[:, HALF:]]
    pieces += [jnp.where(is_left, tops[0], tops[1]), jnp.where(is_left, tops[1], tops[0])]
    pieces += [jnp.zeros((TAIL - ROW_MASK - 2, HALF), jnp.float32)]
    message_ref[TSIDE : TSIDE + TAIL, :] = jnp.concatenate(pieces, axis=0)


def unpack_kernel(keep_ref, got_ref, cell_ref, fac_ref):
    core = lax.axis_index("tile") % 2
    for side, ref in ((core, keep_ref), (1 - core, got_ref)):
        rows = pl.ds(pl.multiple_of(side * COLS_HALF, COLS_HALF), COLS_HALF)
        cell_ref[rows, :HALF] = ref[:COLS_HALF, :]
        cell_ref[rows, HALF:] = ref[COLS_HALF:TSIDE, :]
    tail = keep_ref[TSIDE:, :]
    total = log_add(tail[ROW_POT : ROW_POT + 2], got_ref[TSIDE + ROW_POT : TSIDE + ROW_POT + 2, :])
    fac = tail[ROW_CAP : ROW_CAP + 2] - total
    fac_ref[:, :HALF] = fac[0:1]
    fac_ref[:, HALF:] = fac[1:2]


def early_kernel(neighbor, *refs):
    message_ref, factors, sums_ref = refs[0], refs[1:4], refs[4]
    gathered = Gathered([message_ref] * STEP)
    for line in range(message_ref.shape[0]):
        slot = line * STEP + neighbor
        top = block_top(gathered.potential, factors, slot)
        sums_ref[line] = block_sums(gathered.potential, factors, top, slot)


def first_kernel(*refs):
    gathered = Gathered(refs[:STEP])
    factors = refs[STEP : STEP + 3]
    early_refs = refs[STEP + 3 : STEP + 3 + EARLY]
    part_ref, mask_ref, demand_ref, cap_ref, acc_ref = refs[STEP + 3 + EARLY :]
    build_mask(gathered, lax.axis_index("tile"), mask_ref)
    for slot in gathered.slots:
        demand_ref[:, slot, :] = gathered.demand(slot)
        cap_ref[slot : slot + 1, :] = gathered.capacity(slot)
    base = column_base(row_pass(gathered.potential, factors, mask_ref, demand_ref, acc_ref, early_refs))
    for slot in gathered.slots:
        part_ref[slot : slot + 1, :] = column_part(factors, mask_ref, base, slot)


def second_kernel(*refs):
    factors = refs[:3]
    mask_ref, demand_ref, cap_ref, mine_ref, other_ref, keep_ref, send_ref, pot_ref, acc_ref = refs[3:]
    me = lax.axis_index("tile")
    core = me % 2
    slots = mask_ref.shape[0]
    other = other_ref[...]
    even = lax.broadcasted_iota(jnp.int32, other.shape, 0) % 2 == 0
    swapped = jnp.where(even, pltpu.roll(other, slots - 1, 0), pltpu.roll(other, 1, 0))
    pot_ref[...] = cap_ref[...] - log_add(mine_ref[...], swapped)

    def potential(slot):
        return pot_ref[slot : slot + 1, :]

    shifted = row_pass(potential, factors, mask_ref, demand_ref, acc_ref)
    acc_ref[...] = shifted
    base = column_base(shifted)
    x_mid = (core * HALF).astype(jnp.float32) + 0.5 * HALF
    dx = lax.broadcasted_iota(jnp.int32, (1, HALF), 1).astype(jnp.float32) - 0.5 * (HALF - 1)
    dy = lax.broadcasted_iota(jnp.int32, (TSIDE, 1), 0).astype(jnp.float32) - 0.5 * (TSIDE - 1)
    for slot, out_ref in ((0, keep_ref), (1, send_ref)):
        y_mid = ((me ^ slot) * TSIDE).astype(jnp.float32) + 0.5 * TSIDE
        lift = (dx * (dx + 2.0 * (x_mid - MIDDLE)) + dy * (dy + 2.0 * (y_mid - MIDDLE))) * SCALE
        for start in (0, COLS_HALF):
            rows = slice(start, start + COLS_HALF)
            out_ref[rows, :] = swap_tile(acc_ref[rows, slot, :] + lift[rows])
        part = column_part(factors, mask_ref, base, slot)
        cap = cap_ref[slot : slot + 1, :]
        pieces = [part[:, :HALF], part[:, HALF:], cap[:, :HALF], cap[:, HALF:]]
        pieces += [jnp.zeros((TAIL - ROW_MASK, HALF), jnp.float32)]
        out_ref[TSIDE:, :] = jnp.concatenate(pieces, axis=0)


def exchange(block, distance):
    devices = lax.axis_size("tile")
    return lax.ppermute(block, "tile", [(i, i ^ distance) for i in range(devices)])


def on_device_all_rows(log_demand, log_capacity, warm_potential, facility_xy, pair_block, pair_count):
    slots = lax.axis_size("tile")
    width = log_capacity.shape[1]
    light = pltpu.CompilerParams(vmem_limit_bytes=4 * 1024 * 1024)
    heavy = pltpu.CompilerParams(vmem_limit_bytes=16 * 1024 * 1024)
    local = (log_demand, log_capacity, warm_potential, pair_block, pair_count.reshape(1, -1))
    local = [pltpu.with_memory_space_constraint(x, pltpu.HBM) for x in local]
    message = pl.pallas_call(
        pack_kernel,
        in_specs=[pl.BlockSpec(memory_space=pltpu.HBM)] * len(local),
        out_shape=jax.ShapeDtypeStruct((ROWS, HALF), jnp.float32),
        scratch_shapes=[pltpu.VMEM(x.shape, x.dtype) for x in local]
        + [pltpu.SemaphoreType.DMA((len(local),))],
        compiler_params=light,
        name="pack",
    )(*local)
    factors = pl.pallas_call(
        lambda *refs: setup_kernel(slots, *refs),
        out_shape=(
            jax.ShapeDtypeStruct((slots, 2 * HALF, width), jnp.bfloat16),
            jax.ShapeDtypeStruct((slots, TSIDE, SUBLANES, width), jnp.float32),
            jax.ShapeDtypeStruct((slots, slots, width), jnp.float32),
        ),
        compiler_params=light,
        name="setup",
    )(facility_xy)
    lines = message[None]
    lines = jnp.concatenate([lines] + [exchange(lines, STEP * i) for i in range(1, slots // STEP)], axis=0)
    same = lines[:, :KEEP_ROWS]
    across = lines[:, TSIDE:]
    gathered = (lines, exchange(across, 1), exchange(same, 2), exchange(across, 3))
    early = [
        pl.pallas_call(
            lambda *refs, neighbor=neighbor: early_kernel(neighbor, *refs),
            out_shape=jax.ShapeDtypeStruct((slots // STEP, TSIDE, slots, HALF), jnp.float32),
            compiler_params=heavy,
            name="early",
        )(gathered[neighbor], *factors)
        for neighbor in range(EARLY)
    ]
    part, mask, demand, cap = pl.pallas_call(
        first_kernel,
        out_shape=(
            jax.ShapeDtypeStruct((slots, width), jnp.float32),
            jax.ShapeDtypeStruct((slots, slots, HALF), jnp.float32),
            jax.ShapeDtypeStruct((TSIDE, slots, HALF), jnp.float32),
            jax.ShapeDtypeStruct((slots, width), jnp.float32),
        ),
        scratch_shapes=[pltpu.VMEM((TSIDE, slots, HALF), jnp.float32)],
        compiler_params=heavy,
        name="first_iteration",
    )(*gathered, *factors, *early)
    other = exchange(part, 1)
    keep, send = pl.pallas_call(
        second_kernel,
        out_shape=(
            jax.ShapeDtypeStruct((KEEP_ROWS, HALF), jnp.float32),
            jax.ShapeDtypeStruct((KEEP_ROWS, HALF), jnp.float32),
        ),
        scratch_shapes=[
            pltpu.VMEM((slots, width), jnp.float32),
            pltpu.VMEM((TSIDE, slots, HALF), jnp.float32),
        ],
        compiler_params=heavy,
        name="second_iteration",
    )(*factors, mask, demand, cap, part, other)
    got = exchange(send, 1)
    return pl.pallas_call(
        unpack_kernel,
        out_shape=(
            jax.ShapeDtypeStruct(log_demand.shape, jnp.float32),
            jax.ShapeDtypeStruct(log_capacity.shape, jnp.float32),
        ),
        compiler_params=light,
        name="unpack",
    )(keep, got)


def from_behind(block, axis, distance):
    devices = range(lax.axis_size(axis))
    route = [(i - distance, i) for i in devices if i - distance in devices]
    return lax.ppermute(block, axis, route)


def cell_coords(tile_index):
    cell_ids = jnp.arange(TSIDE * TSIDE, dtype=jnp.int32)
    column = tile_index % TILE_COLS * TSIDE + cell_ids % TSIDE
    row_cell = tile_index // TILE_COLS * TSIDE + cell_ids // TSIDE
    return (column.astype(jnp.float32) + 0.5, row_cell.astype(jnp.float32) + 0.5)


def pair_cost(coord_x, coord_y, positions):
    delta_x = coord_x[None, :, None] - positions[:, 0, :][:, None, :]
    delta_y = coord_y[None, :, None] - positions[:, 1, :][:, None, :]
    return (delta_x * delta_x + delta_y * delta_y) / float(REACH * REACH)


def tile_pass(tile_index, demand_row, potentials, positions, active):
    coord_x, coord_y = cell_coords(tile_index)
    pair_costs = pair_cost(coord_x, coord_y, positions)
    scores = jnp.where(active[:, None, None], potentials[:, None, :] - pair_costs, LOWEST)
    row_top = jnp.max(scores, axis=(0, 2))
    row_sum = jnp.sum(jnp.exp(scores - row_top[None, :, None]), axis=(0, 2))
    cell_pot = demand_row - (row_top + jnp.log(row_sum))
    column_scores = cell_pot[None, :, None] - pair_costs
    col_top = jnp.max(column_scores, axis=1)
    col_sum = jnp.sum(jnp.exp(column_scores - col_top[:, None, :]), axis=1)
    col_top = jnp.where(active[:, None], col_top, LOWEST)
    col_sum = jnp.where(active[:, None], col_sum, 0.0)
    return (cell_pot, col_top, col_sum)


def merge_parts(top_a, sum_a, top_b, sum_b):
    top_new = jnp.maximum(top_a, top_b)
    return (top_new, sum_a * jnp.exp(top_a - top_new) + sum_b * jnp.exp(top_b - top_new))


def on_device(log_demand, log_capacity, warm_potential, facility_xy, pair_block, pair_count):
    tiles_here = log_demand.shape[0]
    blocks_here = log_capacity.shape[0]
    block_width = log_capacity.shape[1]
    devices_along = lax.axis_size("tile")
    my_index = lax.axis_index("tile")
    reach = min(devices_along - 1, (SPAN + blocks_here - 1) // blocks_here)
    window = 2 * reach + 1
    tile_ids = my_index * tiles_here + jnp.arange(tiles_here, dtype=jnp.int32)
    slot_ids = jnp.arange(KSLOTS, dtype=jnp.int32)
    first_block = (my_index - reach) * blocks_here
    local_block = pair_block - first_block
    facility_pot = warm_potential
    cell_pot = log_demand
    for step_index in range(ITERS):
        slabs = []
        for position in range(window):
            distance = reach - position
            if distance == 0:
                slabs.append(facility_pot)
            else:
                slabs.append(from_behind(facility_pot, "tile", distance))
        window_pot = jnp.concatenate(slabs, axis=0)

        def one_tile(inputs):
            tile_index, demand_row, blocks, nearby, slot_limit = inputs
            active = slot_ids < slot_limit
            return tile_pass(
                tile_index, demand_row, window_pot[nearby], facility_xy[blocks], active
            )

        cell_pot, col_top, col_sum = lax.map(
            one_tile, (tile_ids, log_demand, pair_block, local_block, pair_count)
        )
        flat_ids = local_block.reshape(-1)
        flat_top = col_top.reshape(-1, block_width)
        flat_sum = col_sum.reshape(-1, block_width)
        local_top = (
            jnp.full((window * blocks_here, block_width), LOWEST, jnp.float32)
            .at[flat_ids]
            .max(flat_top)
        )
        local_sum = (
            jnp.zeros((window * blocks_here, block_width), jnp.float32)
            .at[flat_ids]
            .add(flat_sum * jnp.exp(flat_top - local_top[flat_ids]))
        )

        def slab_of(position):
            return (
                local_top[position * blocks_here : (position + 1) * blocks_here],
                local_sum[position * blocks_here : (position + 1) * blocks_here],
            )

        own_top, block_sum = slab_of(reach)
        for distance in range(-reach, reach + 1):
            if distance != 0:
                send_top, send_sum = slab_of(reach + distance)
                got_top, got_sum = from_behind((send_top, send_sum), "tile", distance)
                source = my_index - distance
                valid = (source >= 0) & (source < devices_along)
                got_top = jnp.where(valid, got_top, LOWEST)
                got_sum = jnp.where(valid, got_sum, 0.0)
                own_top, block_sum = merge_parts(own_top, block_sum, got_top, got_sum)
        facility_pot = log_capacity - (own_top + jnp.log(block_sum))
    return (cell_pot, facility_pot)


def solution(mesh):
    placed = (
        P(("groups", "tile"), None),
        P(("groups", "tile"), None),
        P(("groups", "tile"), None),
        P("groups", None, None),
        P(("groups", "tile"), None),
        P(("groups", "tile")),
    )
    devices = mesh.shape["tile"]
    small = devices % 2 == 0 and devices * COLS_HALF == HALF

    def program(log_demand, log_capacity, warm_potential, facility_xy, pair_block, pair_count):
        one_row = log_demand.shape[0] == mesh.size * TILE_COLS and log_capacity.shape[0] == mesh.size
        fits = small and one_row and log_capacity.shape[1] == 2 * HALF
        body = on_device_all_rows if fits else on_device
        return jax.shard_map(
            body,
            mesh=mesh,
            in_specs=placed,
            out_specs=(P(("groups", "tile"), None), P(("groups", "tile"), None)),
            check_vma=False,
        )(log_demand, log_capacity, warm_potential, facility_xy, pair_block, pair_count)

    return program
```

```python
import jax
import jax.numpy as jnp
from jax import lax
from jax.experimental import pallas as pl
from jax.experimental.pallas import tpu as pltpu
from jax.sharding import PartitionSpec as P

TSIDE = 16
TILE_COLS = 16
KSLOTS = 16
ITERS = 2
REACH = 64
SPAN = 16


LOWEST = -1e30

HALF = TSIDE * TILE_COLS // 2
COLS_HALF = TILE_COLS // 2
SCALE = 1.0 / float(REACH * REACH)
MIDDLE = 736.0
TAIL = 8
ROWS = 2 * TSIDE + TAIL
KEEP_ROWS = TSIDE + TAIL
ROW_POT = 0
ROW_CAP = 2
ROW_MASK = 4
STEP = 4
PLACES = (0, 1, 3, 2)
EARLY = 3
SUBLANES = 8
LOG2E = 1.4426950408889634
LN2 = 0.6931471805599453


def dot_nt(a, b):
    return lax.dot_general(a, b, (((1,), (1,)), ((), ())), preferred_element_type=jnp.float32)


def dot_nn(a, b):
    return lax.dot_general(a, b, (((1,), (0,)), ((), ())), preferred_element_type=jnp.float32)


def split(values):
    high = values.astype(jnp.bfloat16)
    low = (values - high.astype(jnp.float32)).astype(jnp.bfloat16)
    return high, low


def halves_of(row_pair):
    return jnp.concatenate([row_pair[0:1, :], row_pair[1:2, :]], axis=1)


class Gathered:
    def __init__(self, refs):
        self.refs = refs
        self.slots = range(len(refs) * refs[0].shape[0])

    def block_of(self, slot, first, rows):
        return self.refs[slot % STEP][PLACES.index(slot // STEP), first : first + rows, :]

    def demand(self, slot):
        return self.block_of(slot, TAIL if slot % 2 else 0, TSIDE)

    def tail(self, slot):
        return self.block_of(slot, 0 if slot % 2 else TSIDE, TAIL)

    def potential(self, slot):
        return halves_of(self.tail(slot)[ROW_POT : ROW_POT + 2])

    def capacity(self, slot):
        return halves_of(self.tail(slot)[ROW_CAP : ROW_CAP + 2])

    def mask(self, slot):
        row = ROW_MASK + slot % 2
        return self.tail(slot)[row : row + 1]


def setup_kernel(slots, xy_ref, xf_ref, yf_ref, cost_ref):
    me = lax.axis_index("tile")
    x_mid = (me % 2 * HALF).astype(jnp.float32) + 0.5 * HALF
    row_ids = me ^ lax.broadcasted_iota(jnp.int32, (slots, 1), 0)
    y_mid = (row_ids * TSIDE).astype(jnp.float32) + 0.5 * TSIDE
    x_off = lax.broadcasted_iota(jnp.int32, (HALF, 1), 0).astype(jnp.float32) - 0.5 * (HALF - 1)
    y_off = lax.broadcasted_iota(jnp.int32, (TSIDE, 1), 0).astype(jnp.float32) - 0.5 * (TSIDE - 1)
    for slot in range(slots):
        block = me ^ slot
        fx = xy_ref[block, 0:1, :]
        fy = xy_ref[block, 1:2, :]
        high, low = split(jnp.exp(x_off * ((fx - MIDDLE) * (2.0 * SCALE))))
        xf_ref[slot, :HALF, :] = high
        xf_ref[slot, HALF:, :] = low
        y_factor = jnp.exp(y_off * ((fy - MIDDLE) * (2.0 * SCALE)))
        yf_ref[slot] = jnp.broadcast_to(y_factor[:, None, :], yf_ref.shape[1:])
        dx = x_mid - fx
        dy = y_mid - fy
        cost_ref[slot] = (dx * dx + dy * dy) * SCALE


def build_mask(gathered, me, mask_ref):
    slots = len(gathered.slots)
    marks = jnp.concatenate([gathered.mask(slot) for slot in gathered.slots], axis=0)
    lane_block = lax.broadcasted_iota(jnp.int32, (slots, slots, HALF), 2) // COLS_HALF
    own_block = lax.broadcasted_iota(jnp.int32, (slots, slots, HALF), 0) ^ me
    picked = jnp.where(lane_block == own_block, marks[None], 0.0)
    picked = picked.reshape(slots * slots, HALF).astype(jnp.bfloat16)
    source = lax.broadcasted_iota(jnp.int32, (HALF, HALF), 0) % COLS_HALF
    target = lax.broadcasted_iota(jnp.int32, (HALF, HALF), 1) // TSIDE
    spread = jnp.where(source == target, 1.0, 0.0).astype(jnp.bfloat16)
    mask_ref[...] = dot_nn(picked, spread).reshape(slots, slots, HALF)


def block_top(potential, factors, slot):
    return jnp.max(potential(slot) - factors[2][slot], axis=1, keepdims=True)


def block_sums(potential, factors, top, slot):
    xf_ref, yf_ref, cost_ref = factors
    slots = top.shape[0]
    weight = jnp.exp(potential(slot) - cost_ref[slot] - top)
    parts = [weight[i : i + SUBLANES][None] * yf_ref[slot] for i in range(0, slots, SUBLANES)]
    lhs = jnp.concatenate(parts, axis=1)
    a_high, a_low = split(lhs.reshape(TSIDE * slots, lhs.shape[-1]))
    return row_product(a_high, a_low, xf_ref, slot).reshape(TSIDE, slots, HALF)


def row_pass(potential, factors, mask_ref, demand_ref, acc_ref, early_refs=()):
    slots = mask_ref.shape[0]
    best = jnp.full((slots, HALF), LOWEST, jnp.float32)
    tops = []
    for slot in range(slots):
        top = block_top(potential, factors, slot)
        tops.append(top)
        best = jnp.maximum(best, jnp.where(mask_ref[slot] > 0.0, top, LOWEST))
    for slot in range(slots):
        top = tops[slot]
        if slot % STEP < len(early_refs):
            part = early_refs[slot % STEP][slot // STEP]
        else:
            part = block_sums(potential, factors, top, slot)
        scale = jnp.where(mask_ref[slot] > 0.0, jnp.exp(jnp.minimum(top - best, 0.0)), 0.0)
        scaled = part * scale[None]
        if slot == 0:
            acc_ref[...] = scaled
        else:
            acc_ref[...] += scaled
    return demand_ref[...] - best[None] - jnp.log(acc_ref[...])


def row_product(a_high, a_low, xf_ref, slot):
    both = dot_nt(a_high, xf_ref[slot])
    third = dot_nt(a_low, xf_ref[slot, :HALF, :])
    return both[:, :HALF] + both[:, HALF:] + third


def column_product(w_high, w_low, xf_ref, slot):
    mixed = dot_nn(jnp.concatenate([w_high, w_high], axis=1), xf_ref[slot])
    return mixed + dot_nn(w_low, xf_ref[slot, :HALF, :])


def column_base(shifted):
    scaled = shifted * LOG2E
    level = jnp.ceil(jnp.max(scaled, axis=0))
    high, low = split(jnp.exp2(scaled - level[None]))
    return level, high, low


def column_part(factors, mask_ref, base, slot):
    xf_ref, yf_ref, cost_ref = factors
    level, high, low = base
    slots = level.shape[0]
    active = mask_ref[slot] > 0.0
    top = jnp.max(jnp.where(active, level, LOWEST), axis=1, keepdims=True)
    scale = jnp.where(active, jnp.exp2(jnp.minimum(level - top, 0.0)), 0.0).astype(jnp.bfloat16)
    w_high = (high * scale[None]).reshape(TSIDE * slots, HALF)
    w_low = (low * scale[None]).reshape(TSIDE * slots, HALF)
    mixed = column_product(w_high, w_low, xf_ref, slot)
    mixed = mixed.reshape(TSIDE, slots, mixed.shape[-1])
    sums = [
        jnp.sum(mixed[:, i : i + SUBLANES] * yf_ref[slot], axis=0) for i in range(0, slots, SUBLANES)
    ]
    sums = jnp.concatenate(sums, axis=0)
    tops = top * LN2 - cost_ref[slot]
    best = jnp.max(tops, axis=0, keepdims=True)
    total = jnp.sum(sums * jnp.exp(tops - best), axis=0, keepdims=True)
    return best + jnp.log(total)


def log_add(a, b):
    top = jnp.maximum(a, b)
    return top + jnp.log(jnp.exp(a - top) + jnp.exp(b - top))


def swap_tile(values):
    row = lax.broadcasted_iota(jnp.int32, (COLS_HALF, HALF), 0)
    group = lax.broadcasted_iota(jnp.int32, (COLS_HALF, HALF), 1) // TSIDE
    step = 1
    while step < COLS_HALF:
        from_below = pltpu.roll(pltpu.roll(values, COLS_HALF - step, 0), TSIDE * step, 1)
        from_above = pltpu.roll(pltpu.roll(values, step, 0), HALF - TSIDE * step, 1)
        moved = jnp.where((group & step) != 0, from_below, from_above)
        values = jnp.where((row & step) == (group & step), values, moved)
        step *= 2
    return values


def pack_kernel(*refs):
    sources, message_ref, targets, sems = refs[:5], refs[5], refs[6:11], refs[11]
    copies = [
        pltpu.make_async_copy(source, target, sems.at[i])
        for i, (source, target) in enumerate(zip(sources, targets, strict=True))
    ]
    for copy in copies:
        copy.start()
    for copy in copies:
        copy.wait()
    demand_ref, cap_ref, pot_ref, pair_ref, count_ref = targets
    tiles = 2 * COLS_HALF
    tile_of = lax.broadcasted_iota(jnp.int32, (tiles, tiles), 0)
    lane_of = lax.broadcasted_iota(jnp.int32, (tiles, tiles), 1)
    counts = jnp.sum(jnp.where(tile_of == lane_of, count_ref[...], 0), axis=1, keepdims=True)
    pairs = jnp.where(lax.broadcasted_iota(jnp.int32, (tiles, KSLOTS), 1) < counts, pair_ref[...], -1)
    lanes = lax.broadcasted_iota(jnp.int32, (tiles, HALF), 1)
    found = lanes < 0
    for slot in range(KSLOTS):
        found = found | (pairs[:, slot : slot + 1] == lanes // COLS_HALF)
    own = lax.broadcasted_iota(jnp.int32, (tiles, HALF), 0) % COLS_HALF == lanes % COLS_HALF
    marks = jnp.where(found & own, 1.0, 0.0)
    is_left = lax.axis_index("tile") % 2 == 0
    tops = [jnp.sum(marks[start : start + COLS_HALF], axis=0, keepdims=True) for start in (0, COLS_HALF)]
    for start in (0, COLS_HALF):
        lanes_of = slice(start // COLS_HALF * HALF, (start // COLS_HALF + 1) * HALF)
        sides = [swap_tile(demand_ref[i : i + COLS_HALF, lanes_of]) for i in (0, COLS_HALF)]
        message_ref[start : start + COLS_HALF, :] = jnp.where(is_left, sides[0], sides[1])
        below = KEEP_ROWS + start
        message_ref[below : below + COLS_HALF, :] = jnp.where(is_left, sides[1], sides[0])
    pieces = [pot_ref[:, :HALF], pot_ref[:, HALF:], cap_ref[:, :HALF], cap_ref[:, HALF:]]
    pieces += [jnp.where(is_left, tops[0], tops[1]), jnp.where(is_left, tops[1], tops[0])]
    pieces += [jnp.zeros((TAIL - ROW_MASK - 2, HALF), jnp.float32)]
    message_ref[TSIDE : TSIDE + TAIL, :] = jnp.concatenate(pieces, axis=0)


def unpack_kernel(keep_ref, got_ref, cell_ref, fac_ref):
    core = lax.axis_index("tile") % 2
    for side, ref in ((core, keep_ref), (1 - core, got_ref)):
        rows = pl.ds(pl.multiple_of(side * COLS_HALF, COLS_HALF), COLS_HALF)
        cell_ref[rows, :HALF] = ref[:COLS_HALF, :]
        cell_ref[rows, HALF:] = ref[COLS_HALF:TSIDE, :]
    tail = keep_ref[TSIDE:, :]
    total = log_add(tail[ROW_POT : ROW_POT + 2], got_ref[TSIDE + ROW_POT : TSIDE + ROW_POT + 2, :])
    fac = tail[ROW_CAP : ROW_CAP + 2] - total
    fac_ref[:, :HALF] = fac[0:1]
    fac_ref[:, HALF:] = fac[1:2]


def early_kernel(neighbor, *refs):
    message_ref, factors, sums_ref = refs[0], refs[1:4], refs[4]
    gathered = Gathered([message_ref] * STEP)
    for line in range(message_ref.shape[0]):
        slot = line * STEP + neighbor
        top = block_top(gathered.potential, factors, slot)
        sums_ref[line] = block_sums(gathered.potential, factors, top, slot)


def first_kernel(*refs):
    gathered = Gathered(refs[:STEP])
    factors = refs[STEP : STEP + 3]
    early_refs = refs[STEP + 3 : STEP + 3 + EARLY]
    part_ref, mask_ref, demand_ref, cap_ref, acc_ref = refs[STEP + 3 + EARLY :]
    build_mask(gathered, lax.axis_index("tile"), mask_ref)
    for slot in gathered.slots:
        demand_ref[:, slot, :] = gathered.demand(slot)
        cap_ref[slot : slot + 1, :] = gathered.capacity(slot)
    base = column_base(row_pass(gathered.potential, factors, mask_ref, demand_ref, acc_ref, early_refs))
    for slot in gathered.slots:
        part_ref[slot : slot + 1, :] = column_part(factors, mask_ref, base, slot)


def second_kernel(*refs):
    factors = refs[:3]
    mask_ref, demand_ref, cap_ref, mine_ref, other_ref, keep_ref, send_ref, pot_ref, acc_ref = refs[3:]
    me = lax.axis_index("tile")
    core = me % 2
    slots = mask_ref.shape[0]
    other = other_ref[...]
    even = lax.broadcasted_iota(jnp.int32, other.shape, 0) % 2 == 0
    swapped = jnp.where(even, pltpu.roll(other, slots - 1, 0), pltpu.roll(other, 1, 0))
    pot_ref[...] = cap_ref[...] - log_add(mine_ref[...], swapped)

    def potential(slot):
        return pot_ref[slot : slot + 1, :]

    shifted = row_pass(potential, factors, mask_ref, demand_ref, acc_ref)
    acc_ref[...] = shifted
    base = column_base(shifted)
    x_mid = (core * HALF).astype(jnp.float32) + 0.5 * HALF
    dx = lax.broadcasted_iota(jnp.int32, (1, HALF), 1).astype(jnp.float32) - 0.5 * (HALF - 1)
    dy = lax.broadcasted_iota(jnp.int32, (TSIDE, 1), 0).astype(jnp.float32) - 0.5 * (TSIDE - 1)
    for slot, out_ref in ((0, keep_ref), (1, send_ref)):
        y_mid = ((me ^ slot) * TSIDE).astype(jnp.float32) + 0.5 * TSIDE
        lift = (dx * (dx + 2.0 * (x_mid - MIDDLE)) + dy * (dy + 2.0 * (y_mid - MIDDLE))) * SCALE
        for start in (0, COLS_HALF):
            rows = slice(start, start + COLS_HALF)
            out_ref[rows, :] = swap_tile(acc_ref[rows, slot, :] + lift[rows])
        part = column_part(factors, mask_ref, base, slot)
        cap = cap_ref[slot : slot + 1, :]
        pieces = [part[:, :HALF], part[:, HALF:], cap[:, :HALF], cap[:, HALF:]]
        pieces += [jnp.zeros((TAIL - ROW_MASK, HALF), jnp.float32)]
        out_ref[TSIDE:, :] = jnp.concatenate(pieces, axis=0)


def exchange(block, distance):
    devices = lax.axis_size("tile")
    return lax.ppermute(block, "tile", [(i, i ^ distance) for i in range(devices)])


def on_device_all_rows(log_demand, log_capacity, warm_potential, facility_xy, pair_block, pair_count):
    slots = lax.axis_size("tile")
    width = log_capacity.shape[1]
    light = pltpu.CompilerParams(vmem_limit_bytes=4 * 1024 * 1024)
    heavy = pltpu.CompilerParams(vmem_limit_bytes=16 * 1024 * 1024)
    local = (log_demand, log_capacity, warm_potential, pair_block, pair_count.reshape(1, -1))
    local = [pltpu.with_memory_space_constraint(x, pltpu.HBM) for x in local]
    message = pl.pallas_call(
        pack_kernel,
        in_specs=[pl.BlockSpec(memory_space=pltpu.HBM)] * len(local),
        out_shape=jax.ShapeDtypeStruct((ROWS, HALF), jnp.float32),
        scratch_shapes=[pltpu.VMEM(x.shape, x.dtype) for x in local]
        + [pltpu.SemaphoreType.DMA((len(local),))],
        compiler_params=light,
        name="pack",
    )(*local)
    factors = pl.pallas_call(
        lambda *refs: setup_kernel(slots, *refs),
        out_shape=(
            jax.ShapeDtypeStruct((slots, 2 * HALF, width), jnp.bfloat16),
            jax.ShapeDtypeStruct((slots, TSIDE, SUBLANES, width), jnp.float32),
            jax.ShapeDtypeStruct((slots, slots, width), jnp.float32),
        ),
        compiler_params=light,
        name="setup",
    )(facility_xy)
    lines = message[None]
    lines = jnp.concatenate([lines] + [exchange(lines, STEP * i) for i in PLACES[1:]], axis=0)
    same = lines[:, :KEEP_ROWS]
    across = lines[:, TSIDE:]
    gathered = (lines, exchange(across, 1), exchange(same, 2), exchange(across, 3))
    early = [
        pl.pallas_call(
            lambda *refs, neighbor=neighbor: early_kernel(neighbor, *refs),
            out_shape=jax.ShapeDtypeStruct((slots // STEP, TSIDE, slots, HALF), jnp.float32),
            compiler_params=heavy,
            name="early",
        )(gathered[neighbor], *factors)
        for neighbor in range(EARLY)
    ]
    part, mask, demand, cap = pl.pallas_call(
        first_kernel,
        out_shape=(
            jax.ShapeDtypeStruct((slots, width), jnp.float32),
            jax.ShapeDtypeStruct((slots, slots, HALF), jnp.float32),
            jax.ShapeDtypeStruct((TSIDE, slots, HALF), jnp.float32),
            jax.ShapeDtypeStruct((slots, width), jnp.float32),
        ),
        scratch_shapes=[pltpu.VMEM((TSIDE, slots, HALF), jnp.float32)],
        compiler_params=heavy,
        name="first_iteration",
    )(*gathered, *factors, *early)
    other = exchange(part, 1)
    keep, send = pl.pallas_call(
        second_kernel,
        out_shape=(
            jax.ShapeDtypeStruct((KEEP_ROWS, HALF), jnp.float32),
            jax.ShapeDtypeStruct((KEEP_ROWS, HALF), jnp.float32),
        ),
        scratch_shapes=[
            pltpu.VMEM((slots, width), jnp.float32),
            pltpu.VMEM((TSIDE, slots, HALF), jnp.float32),
        ],
        compiler_params=heavy,
        name="second_iteration",
    )(*factors, mask, demand, cap, part, other)
    got = exchange(send, 1)
    return pl.pallas_call(
        unpack_kernel,
        out_shape=(
            jax.ShapeDtypeStruct(log_demand.shape, jnp.float32),
            jax.ShapeDtypeStruct(log_capacity.shape, jnp.float32),
        ),
        compiler_params=light,
        name="unpack",
    )(keep, got)


def from_behind(block, axis, distance):
    devices = range(lax.axis_size(axis))
    route = [(i - distance, i) for i in devices if i - distance in devices]
    return lax.ppermute(block, axis, route)


def cell_coords(tile_index):
    cell_ids = jnp.arange(TSIDE * TSIDE, dtype=jnp.int32)
    column = tile_index % TILE_COLS * TSIDE + cell_ids % TSIDE
    row_cell = tile_index // TILE_COLS * TSIDE + cell_ids // TSIDE
    return (column.astype(jnp.float32) + 0.5, row_cell.astype(jnp.float32) + 0.5)


def pair_cost(coord_x, coord_y, positions):
    delta_x = coord_x[None, :, None] - positions[:, 0, :][:, None, :]
    delta_y = coord_y[None, :, None] - positions[:, 1, :][:, None, :]
    return (delta_x * delta_x + delta_y * delta_y) / float(REACH * REACH)


def tile_pass(tile_index, demand_row, potentials, positions, active):
    coord_x, coord_y = cell_coords(tile_index)
    pair_costs = pair_cost(coord_x, coord_y, positions)
    scores = jnp.where(active[:, None, None], potentials[:, None, :] - pair_costs, LOWEST)
    row_top = jnp.max(scores, axis=(0, 2))
    row_sum = jnp.sum(jnp.exp(scores - row_top[None, :, None]), axis=(0, 2))
    cell_pot = demand_row - (row_top + jnp.log(row_sum))
    column_scores = cell_pot[None, :, None] - pair_costs
    col_top = jnp.max(column_scores, axis=1)
    col_sum = jnp.sum(jnp.exp(column_scores - col_top[:, None, :]), axis=1)
    col_top = jnp.where(active[:, None], col_top, LOWEST)
    col_sum = jnp.where(active[:, None], col_sum, 0.0)
    return (cell_pot, col_top, col_sum)


def merge_parts(top_a, sum_a, top_b, sum_b):
    top_new = jnp.maximum(top_a, top_b)
    return (top_new, sum_a * jnp.exp(top_a - top_new) + sum_b * jnp.exp(top_b - top_new))


def on_device(log_demand, log_capacity, warm_potential, facility_xy, pair_block, pair_count):
    tiles_here = log_demand.shape[0]
    blocks_here = log_capacity.shape[0]
    block_width = log_capacity.shape[1]
    devices_along = lax.axis_size("tile")
    my_index = lax.axis_index("tile")
    reach = min(devices_along - 1, (SPAN + blocks_here - 1) // blocks_here)
    window = 2 * reach + 1
    tile_ids = my_index * tiles_here + jnp.arange(tiles_here, dtype=jnp.int32)
    slot_ids = jnp.arange(KSLOTS, dtype=jnp.int32)
    first_block = (my_index - reach) * blocks_here
    local_block = pair_block - first_block
    facility_pot = warm_potential
    cell_pot = log_demand
    for step_index in range(ITERS):
        slabs = []
        for position in range(window):
            distance = reach - position
            if distance == 0:
                slabs.append(facility_pot)
            else:
                slabs.append(from_behind(facility_pot, "tile", distance))
        window_pot = jnp.concatenate(slabs, axis=0)

        def one_tile(inputs):
            tile_index, demand_row, blocks, nearby, slot_limit = inputs
            active = slot_ids < slot_limit
            return tile_pass(
                tile_index, demand_row, window_pot[nearby], facility_xy[blocks], active
            )

        cell_pot, col_top, col_sum = lax.map(
            one_tile, (tile_ids, log_demand, pair_block, local_block, pair_count)
        )
        flat_ids = local_block.reshape(-1)
        flat_top = col_top.reshape(-1, block_width)
        flat_sum = col_sum.reshape(-1, block_width)
        local_top = (
            jnp.full((window * blocks_here, block_width), LOWEST, jnp.float32)
            .at[flat_ids]
            .max(flat_top)
        )
        local_sum = (
            jnp.zeros((window * blocks_here, block_width), jnp.float32)
            .at[flat_ids]
            .add(flat_sum * jnp.exp(flat_top - local_top[flat_ids]))
        )

        def slab_of(position):
            return (
                local_top[position * blocks_here : (position + 1) * blocks_here],
                local_sum[position * blocks_here : (position + 1) * blocks_here],
            )

        own_top, block_sum = slab_of(reach)
        for distance in range(-reach, reach + 1):
            if distance != 0:
                send_top, send_sum = slab_of(reach + distance)
                got_top, got_sum = from_behind((send_top, send_sum), "tile", distance)
                source = my_index - distance
                valid = (source >= 0) & (source < devices_along)
                got_top = jnp.where(valid, got_top, LOWEST)
                got_sum = jnp.where(valid, got_sum, 0.0)
                own_top, block_sum = merge_parts(own_top, block_sum, got_top, got_sum)
        facility_pot = log_capacity - (own_top + jnp.log(block_sum))
    return (cell_pot, facility_pot)


def solution(mesh):
    placed = (
        P(("groups", "tile"), None),
        P(("groups", "tile"), None),
        P(("groups", "tile"), None),
        P("groups", None, None),
        P(("groups", "tile"), None),
        P(("groups", "tile")),
    )
    devices = mesh.shape["tile"]
    small = devices % 2 == 0 and devices * COLS_HALF == HALF

    def program(log_demand, log_capacity, warm_potential, facility_xy, pair_block, pair_count):
        one_row = log_demand.shape[0] == mesh.size * TILE_COLS and log_capacity.shape[0] == mesh.size
        fits = small and one_row and log_capacity.shape[1] == 2 * HALF
        body = on_device_all_rows if fits else on_device
        return jax.shard_map(
            body,
            mesh=mesh,
            in_specs=placed,
            out_specs=(P(("groups", "tile"), None), P(("groups", "tile"), None)),
            check_vma=False,
        )(log_demand, log_capacity, warm_potential, facility_xy, pair_block, pair_count)

    return program
```
